32 devices in a mesh: seq: 16 (over z, x, core), hx: 2 (over y).
Axes of the slice: x: 2, y: 2, z: 4, core: 2. Of those that a mesh axis runs over, the one named last changes fastest.
Arguments:
- stream: float32 [16, 2048, 768], P('seq', 'hx'), may hold values from -6 to 6
- cotangent: float32 [16, 2048, 768], P('seq', 'hx'), may hold values from -6 to 6
- norm_gain: bfloat16 [768], P('seq'), may hold values from 0.5 to 1.5
- in_main: bfloat16 [768, 3328], P('seq'), may hold values from -0.21875 to 0.21875
- in_dt: bfloat16 [768, 24], P('seq'), may hold values from -0.21875 to 0.21875
- conv_weight: bfloat16 [4, 1792], P(None, 'seq'), may hold values from -3 to 3
- conv_bias: bfloat16 [1792], P('seq'), may hold values from -3 to 3
- dt_bias: float32 [24], replicated, may hold values from -6.9 to -2.25
- a_log: float32 [24], replicated, may hold values from 0 to 2.77
- skip_gain: float32 [24], replicated, may hold values from 0.5 to 2
- gated_gain: bfloat16 [1536], P('seq'), may hold values from 0.5 to 1.5
- out_weight: bfloat16 [1536, 768], P('seq'), may hold values from -0.15625 to 0.15625
Outputs:
- output: float32 [16, 2048, 768], P('seq', 'hx')
- grad_stream: float32 [16, 2048, 768], P('seq', 'hx')
- grad_norm_gain: float32 [768], P('seq')
- grad_in_main: float32 [768, 3328], P('seq')
- grad_in_dt: float32 [768, 24], P('seq')
- grad_conv_weight: float32 [4, 1792], P(None, 'seq')
- grad_conv_bias: float32 [1792], P('seq')
- grad_dt_bias: float32 [24], replicated
- grad_a_log: float32 [24], replicated
- grad_skip_gain: float32 [24], replicated
- grad_gated_gain: float32 [1536], P('seq')
- grad_out_weight: float32 [1536, 768], P('seq')
The draws below stay inside these ranges and needn't reach their ends.
All inputs are finite; a program needn't handle non-finite values.
Results may differ from the reference program's by a relative error of at most 0.012.
Values may be sent and summed in bfloat16 or wider, within the bound.
No kernel may reach another device: no remote copies, remote signals or barrier semaphores. Data moves between devices by JAX's collectives and lax.ppermute only.
A program may use at most 192 MiB of HBM per device.

```python
import jax
import jax.numpy as jnp
from jax import lax

D = 768
HEADS = 24
STATE = 128
CONV = 4
GROUP = 256
SEQLEN = 2048
DI = 1536
CD = 1792
MAIN = 3328
SEQS = 16


def raised(drawn, rng, source, target, parts, factor):
    def block_of(dim):
        return (jnp.arange(drawn.shape[dim]) // (drawn.shape[dim] // parts)).reshape((-1,) + (1,) * (drawn.ndim - 1 - dim))

    first = jax.random.permutation(rng, parts)[block_of(target)]
    second = (block_of(target) + parts // 2) % parts
    return jnp.where((block_of(source) == first) | (block_of(source) == second), factor * drawn, drawn)


def block_scale(own_key, extent, split, smallest, high):
    gain, own = 1.0, jax.random.fold_in(own_key, 6)
    for axis_at, parts in split:
        draws = jnp.exp(jax.random.uniform(jax.random.fold_in(own, axis_at), (parts,), jnp.float32, smallest / len(split), high / len(split)))
        gain = gain * jnp.repeat(draws, extent[axis_at] // parts).reshape([-1 if axis == axis_at else 1 for axis in range(len(extent))])
    return gain


def noise(rng, extent, deviation, most, split=(), kind=jnp.bfloat16):
    gain = block_scale(rng, extent, split, -0.22, 0.18) if split else 1.0
    drawn = jax.random.normal(rng, extent, jnp.float32) * deviation * gain
    return jnp.minimum(jnp.maximum(drawn, -most), most).astype(kind)


def noise_with(rng, shape, deviation, reach, split, heavy, kind=jnp.bfloat16):
    values = deviation * jax.random.normal(rng, shape, jnp.float32)
    if split:
        values = values * block_scale(rng, shape, split, -0.22, 0.18)
    return jnp.clip(raised(values, jax.random.fold_in(rng, 3), *heavy), -reach, reach).astype(kind)


def setup_inputs(seed: int = 0) -> dict:
    key_of = jax.random.split(jax.random.key(seed), 13)
    stream = noise_with(key_of[0], (SEQS, SEQLEN, D), 1.0, 6.0, ((0, 16), (1, 2)), (0, 2, 16, 2.0), jnp.float32)
    cotangent = noise(key_of[1], (SEQS, SEQLEN, D), 1.0, 6.0, ((0, 16), (1, 2)), jnp.float32)
    norm_gain = jnp.clip(1.0 + 0.1 * jax.random.normal(key_of[2], (D,), jnp.float32), 0.5, 1.5).astype(jnp.bfloat16)
    in_main = noise(key_of[3], (D, MAIN), D ** -0.5, 0.21875, ((0, 16),))
    in_dt = noise(key_of[4], (D, HEADS), D ** -0.5, 0.21875, ((0, 16),))
    conv_weight = noise(key_of[5], (CONV, CD), CONV ** -0.5, 3.0, ((1, 16),))
    conv_bias = noise(key_of[6], (CD,), 0.5, 3.0, ((0, 16),))
    dt_bias = jnp.clip(jax.random.uniform(key_of[7], (HEADS,), jnp.float32, -6.9, -2.25), -6.9, -2.25)
    a_log = jnp.clip(jax.random.uniform(key_of[8], (HEADS,), jnp.float32, 0.0, 2.77), 0.0, 2.77)
    skip_gain = jnp.clip(jax.random.uniform(key_of[9], (HEADS,), jnp.float32, 0.5, 2.0), 0.5, 2.0)
    gated_gain = jnp.clip(1.0 + 0.1 * jax.random.normal(key_of[10], (DI,), jnp.float32), 0.5, 1.5).astype(jnp.bfloat16)
    out_weight = noise(key_of[11], (DI, D), DI ** -0.5, 0.15625, ((0, 16),))
    return {"stream": stream, "cotangent": cotangent, "norm_gain": norm_gain, "in_main": in_main, "in_dt": in_dt, "conv_weight": conv_weight, "conv_bias": conv_bias, "dt_bias": dt_bias, "a_log": a_log, "skip_gain": skip_gain, "gated_gain": gated_gain, "out_weight": out_weight}


EPSILON = 1e-05
PRECISE = lax.Precision.HIGHEST

def conv_silu(pre_conv, kernel, bias_vec):
    length = pre_conv.shape[0]
    padded = jnp.concatenate([jnp.zeros((CONV - 1, pre_conv.shape[1]), pre_conv.dtype), pre_conv], axis=0)
    summed = bias_vec[None, :] + kernel[0][None, :] * padded[0:length]
    for offset in range(1, CONV):
        summed = summed + kernel[offset][None, :] * padded[offset:offset + length]
    return jax.nn.silu(summed)

def block_scan(x_heads, step_size, decay, b_rows, c_rows, skip_vec):
    length, head_count, head_dim = x_heads.shape
    blocks = length // GROUP
    x_blocks = x_heads.reshape(blocks, GROUP, head_count, head_dim)
    step_blocks = step_size.reshape(blocks, GROUP, head_count)
    decay_blocks = decay.reshape(blocks, GROUP, head_count)
    b_blocks = b_rows.reshape(blocks, GROUP, STATE)
    c_blocks = c_rows.reshape(blocks, GROUP, STATE)
    row_index = lax.broadcasted_iota(jnp.int32, (GROUP, GROUP), 0)
    col_index = lax.broadcasted_iota(jnp.int32, (GROUP, GROUP), 1)
    lower_mask = (row_index >= col_index)[:, :, None]

    def advance(state_now, block):
        x_block, step_block, decay_block, b_block, c_block = block
        cumulative = jnp.cumsum(decay_block, axis=0)
        gap_matrix = cumulative[:, None, :] - cumulative[None, :, :]
        within = jnp.where(lower_mask, jnp.exp(jnp.where(lower_mask, gap_matrix, 0.0)), 0.0)
        c_dot_b = jnp.dot(c_block, b_block.T, precision=PRECISE)
        weights_mix = c_dot_b[:, :, None] * within * step_block[None, :, :]
        intra_part = jnp.einsum('tsh,shp->thp', weights_mix, x_block, precision=PRECISE)
        inter_part = jnp.einsum('tn,hpn->thp', c_block, state_now, precision=PRECISE) * jnp.exp(cumulative)[:, :, None]
        tail_weight = jnp.exp(cumulative[-1][None, :] - cumulative) * step_block
        new_state = jnp.exp(cumulative[-1])[:, None, None] * state_now + jnp.einsum('shp,sn->hpn', tail_weight[:, :, None] * x_block, b_block, precision=PRECISE)
        result = intra_part + inter_part + skip_vec[None, :, None] * x_block
        return (new_state, result)
    initial = jnp.zeros((head_count, head_dim, STATE), x_heads.dtype)
    final_state, outputs = lax.scan(jax.checkpoint(advance), initial, (x_blocks, step_blocks, decay_blocks, b_blocks, c_blocks))
    return outputs.reshape(length, head_count * head_dim)

def mixer(conv_in, dt_raw, kernel, bias_vec, step_bias, decay_log, skip_vec):
    length = conv_in.shape[0]
    head_count = dt_raw.shape[1]
    inner_width = conv_in.shape[1] - 2 * STATE
    head_dim = inner_width // head_count
    conv_out = conv_silu(conv_in, kernel, bias_vec)
    x_heads = conv_out[:, :inner_width].reshape(length, head_count, head_dim)
    b_rows = conv_out[:, inner_width:inner_width + STATE]
    c_rows = conv_out[:, inner_width + STATE:]
    step_size = jax.nn.softplus(dt_raw + step_bias[None, :])
    decay = -jnp.exp(decay_log)[None, :] * step_size
    return block_scan(x_heads, step_size, decay, b_rows, c_rows, skip_vec)

def reference(stream, cotangent, norm_gain, in_main, in_dt, conv_weight, conv_bias, dt_bias, a_log, skip_gain, gated_gain, out_weight):
    gain_in = norm_gain.astype(jnp.float32)
    kernel = conv_weight.astype(jnp.float32)
    bias_vec = conv_bias.astype(jnp.float32)
    gain_gate = gated_gain.astype(jnp.float32)

    def one_sequence(totals, inputs_pair):
        tokens_in, tokens_cot = inputs_pair
        root_inv = lax.rsqrt(lax.optimization_barrier(jnp.mean(tokens_in * tokens_in, axis=-1, keepdims=True)) + EPSILON)
        normed = (tokens_in * root_inv * gain_in).astype(jnp.bfloat16)
        projected = jnp.dot(normed, in_main, preferred_element_type=jnp.float32)
        gate_z = projected[:, :DI]
        conv_in = lax.optimization_barrier(projected[:, DI:].astype(jnp.bfloat16)).astype(jnp.float32)
        dt_raw = lax.optimization_barrier(jnp.dot(normed, in_dt, preferred_element_type=jnp.float32).astype(jnp.bfloat16)).astype(jnp.float32)
        scanned_full, pull_back = jax.vjp(mixer, conv_in, dt_raw, kernel, bias_vec, dt_bias, a_log, skip_gain)
        scanned = lax.optimization_barrier(scanned_full.astype(jnp.bfloat16)).astype(jnp.float32)
        sigmoid_z = jax.nn.sigmoid(gate_z)
        silu_z = gate_z * sigmoid_z
        gated = scanned * silu_z
        gate_inv = lax.rsqrt(lax.optimization_barrier(jnp.mean(gated * gated, axis=-1, keepdims=True)) + EPSILON)
        mixed = (gated * gate_inv * gain_gate).astype(jnp.bfloat16)
        output = tokens_in + jnp.dot(mixed, out_weight, preferred_element_type=jnp.float32)
        cot_b = tokens_cot.astype(jnp.bfloat16)
        g_out_weight = lax.dot_general(mixed, cot_b, (((0,), (0,)), ((), ())), preferred_element_type=jnp.float32)
        d_mixed = lax.dot_general(cot_b, out_weight, (((1,), (1,)), ((), ())), preferred_element_type=jnp.float32)
        g_gated_gain = lax.optimization_barrier(jnp.sum(d_mixed * gated * gate_inv, axis=0))
        weighted = gain_gate * d_mixed
        d_gated = gate_inv * weighted - gated * gate_inv ** 3 * lax.optimization_barrier(jnp.mean(weighted * gated, axis=-1, keepdims=True))
        d_scanned = (d_gated * silu_z).astype(jnp.bfloat16)
        d_gate_z = d_gated * scanned * sigmoid_z * (1.0 + gate_z * (1.0 - sigmoid_z))
        d_conv_in, d_dt_raw, g_kernel, g_bias, g_step_bias, g_decay_log, g_skip = pull_back(d_scanned.astype(jnp.float32))
        d_projected = jnp.concatenate([d_gate_z, d_conv_in], axis=1).astype(jnp.bfloat16)
        d_dt_b = d_dt_raw.astype(jnp.bfloat16)
        g_in_main = lax.dot_general(normed, d_projected, (((0,), (0,)), ((), ())), preferred_element_type=jnp.float32)
        g_in_dt = lax.dot_general(normed, d_dt_b, (((0,), (0,)), ((), ())), preferred_element_type=jnp.float32)
        d_normed = lax.dot_general(d_projected, in_main, (((1,), (1,)), ((), ())), preferred_element_type=jnp.float32)
        d_normed = d_normed + lax.dot_general(d_dt_b, in_dt, (((1,), (1,)), ((), ())), preferred_element_type=jnp.float32)
        weighted_in = gain_in * d_normed
        g_norm_gain = lax.optimization_barrier(jnp.sum(d_normed * tokens_in * root_inv, axis=0))
        grad_in = tokens_cot + root_inv * weighted_in - tokens_in * root_inv ** 3 * lax.optimization_barrier(jnp.mean(weighted_in * tokens_in, axis=-1, keepdims=True))
        grads = (g_norm_gain, g_in_main, g_in_dt, g_kernel, g_bias, g_step_bias, g_decay_log, g_skip, g_gated_gain, g_out_weight)
        totals = jax.tree.map(lambda left, right: left + right, totals, grads)
        return (totals, (output, grad_in))
    zeros_init = (jnp.zeros((D,), jnp.float32), jnp.zeros((D, MAIN), jnp.float32), jnp.zeros((D, HEADS), jnp.float32), jnp.zeros((CONV, CD), jnp.float32), jnp.zeros((CD,), jnp.float32), jnp.zeros((HEADS,), jnp.float32), jnp.zeros((HEADS,), jnp.float32), jnp.zeros((HEADS,), jnp.float32), jnp.zeros((DI,), jnp.float32), jnp.zeros((DI, D), jnp.float32))
    totals, results = lax.scan(one_sequence, zeros_init, (stream, cotangent))
    return (results[0], results[1], totals[0], totals[1], totals[2], totals[3], totals[4], totals[5], totals[6], totals[7], totals[8], totals[9])
```

```python
import functools

import jax
import jax.numpy as jnp
from jax import lax
from jax.experimental import pallas as pl
from jax.experimental.pallas import tpu as pltpu
from jax.sharding import PartitionSpec as P

STATE = 128
CONV = 4
EPSILON = 1e-05
Q = 128
LANES = 128
HALO = 16
BF = jnp.bfloat16
F32 = jnp.float32
EXACT = lax.Precision.HIGHEST


def dot(a, b, precision=None):
    return lax.dot_general(
        a, b, (((1,), (0,)), ((), ())), precision=precision, preferred_element_type=F32
    )


def dot_nt(a, b):
    return lax.dot_general(a, b, (((1,), (1,)), ((), ())), preferred_element_type=F32)


def dot_tn(a, b):
    return lax.dot_general(a, b, (((0,), (0,)), ((), ())), preferred_element_type=F32)


def expand(v, ee):
    hi = v.astype(BF)
    lo = (v - hi.astype(F32)).astype(BF)
    return dot(jnp.concatenate([hi, lo], axis=1), ee)


def expand_row(v, ee):
    return expand(jnp.broadcast_to(v, (8, v.shape[1])), ee)[0:1]


def softplus(v):
    return jnp.maximum(v, 0.0) + jnp.log1p(jnp.exp(-jnp.abs(v)))


def sigmoid(v):
    return 1.0 / (1.0 + jnp.exp(-v))


def root_of(v):
    return lax.rsqrt(jnp.mean(v * v, axis=-1, keepdims=True) + EPSILON)


def tri(rows, cols, keep):
    r = lax.broadcasted_iota(jnp.int32, (rows, cols), 0)
    c = lax.broadcasted_iota(jnp.int32, (rows, cols), 1)
    return keep(r, c)


def half_blocks(v, width):
    lane = lax.broadcasted_iota(jnp.int32, v.shape, 1)
    zero = jnp.zeros_like(v)
    return jnp.concatenate([jnp.where(lane < width, v, zero), jnp.where(lane >= width, v, zero)], axis=0)


def project_kernel(
    di,
    halo_ref,
    s_ref,
    gain_ref,
    w_ref,
    cw_ref,
    cb_ref,
    hp_ref,
    ee_ref,
    nrm_ref,
    cin_ref,
    xc_ref,
    dtv_ref,
    cum_ref,
    base_ref,
    sloc_ref,
    fin_ref,
    tot_ref,
    full,
    state,
    base,
):
    i = pl.program_id(0)
    cd = cin_ref.shape[1]

    @pl.when(i == 0)
    def _():
        h = halo_ref[...]
        nh = (h * root_of(h) * gain_ref[...]).astype(BF)
        ph = dot(nh, w_ref[:, :cd]).astype(BF)
        nrm_ref[...] = jnp.zeros_like(nrm_ref)
        nrm_ref[Q - HALO :, :] = nh
        cin_ref[...] = jnp.zeros_like(cin_ref)
        cin_ref[Q - HALO :, :] = ph
        full[0:8, :] = ph.astype(F32)[HALO - 8 :]
        state[...] = jnp.zeros_like(state)
        base[...] = jnp.zeros_like(base)

    @pl.when(i > 0)
    def _():
        s = s_ref[...]
        nrm = (s * root_of(s) * gain_ref[...]).astype(BF)
        nrm_ref[...] = nrm
        proj = dot(nrm, w_ref[...])
        cin = proj[:, :cd].astype(BF)
        cin_ref[...] = cin
        full[8:, :] = cin.astype(F32)
        summed = cb_ref[...] + cw_ref[0:1, :] * full[5 : 5 + Q, :]
        for k in range(1, CONV):
            summed = summed + cw_ref[k : k + 1, :] * full[5 + k : 5 + k + Q, :]
        full[0:8, :] = full[Q : Q + 8, :]
        xc = summed * sigmoid(summed)
        xcb = xc.astype(BF)
        xc_ref[...] = xcb
        dtv = proj[:, cd:].astype(BF).astype(F32) + hp_ref[0:1, :]
        dtv_ref[...] = dtv
        step = softplus(dtv)
        lower = tri(Q, Q, lambda r, c: r >= c).astype(F32)
        cum = dot(lower, hp_ref[1:2, :] * step, EXACT)
        cum_ref[...] = cum
        last = cum[Q - 1 : Q, :]
        base_ref[...] = base[...]
        base[...] = base[...] + last
        sloc_ref[0] = state[...].astype(BF)
        u = (expand(jnp.exp(last - cum) * step, ee_ref[...]) * xc[:, :di]).astype(BF)
        state[...] = state[...] * expand_row(jnp.exp(last), ee_ref[...]) + dot_tn(xcb[:, di : di + STATE], u)

    @pl.when(i == pl.num_programs(0) - 1)
    def _():
        fin_ref[...] = state[...].astype(BF)
        tot_ref[...] = base[...]


def intra_kernel(width, xc_ref, dtv_ref, cum_ref, nrm_ref, wz_ref, skip_ref, ee_ref, yi_ref, z_ref):
    di = yi_ref.shape[1]
    z_ref[...] = dot(nrm_ref[...], wz_ref[...])
    xcb = xc_ref[...]
    x = xcb[:, :di].astype(F32)
    bm, cm = xcb[:, di : di + STATE], xcb[:, di + STATE :]
    cum = cum_ref[...]
    cum_t = cum.T
    mix = jnp.where(tri(Q, Q, lambda r, c: r >= c), dot_nt(cm, bm), 0.0)
    ub = (expand(softplus(dtv_ref[...]), ee_ref[...]) * x).astype(BF)
    for p in range(di // (2 * width)):
        cols = slice(2 * width * p, 2 * width * (p + 1))
        two = []
        for h in (2 * p, 2 * p + 1):
            gap = jnp.minimum(cum[:, h : h + 1] - cum_t[h : h + 1, :], 0.0)
            two.append((jnp.exp(gap) * mix).astype(BF))
        yi_ref[:, cols] = (
            dot(jnp.concatenate(two, axis=1), half_blocks(ub[:, cols], width)) + skip_ref[:, cols] * x[:, cols]
        )


def gate_kernel(
    yi_ref,
    z_ref,
    xc_ref,
    cum_ref,
    base_ref,
    sloc_ref,
    hin_ref,
    s_ref,
    cot_ref,
    wout_ref,
    gain_ref,
    ee_ref,
    out_ref,
    mixed_ref,
    dsc_ref,
    dz_ref,
    gst_ref,
    gst,
):
    i = pl.program_id(0)
    di = yi_ref.shape[1]
    ee = ee_ref[...]
    cm = xc_ref[:, di + STATE :]
    cum = cum_ref[...]
    base = base_ref[0:1, :]
    start = (sloc_ref[0].astype(F32) + expand_row(jnp.exp(base), ee) * hin_ref[...].astype(F32)).astype(BF)
    ex = expand(jnp.exp(cum), ee)
    scanned = (yi_ref[...] + ex * dot(cm, start)).astype(BF).astype(F32)
    z = z_ref[...]
    sig = sigmoid(z)
    silu = z * sig
    gated = scanned * silu
    inv = root_of(gated)
    unit = gated * inv
    mixed = (unit * gain_ref[...]).astype(BF)
    mixed_ref[...] = mixed
    out_ref[...] = s_ref[...] + dot(mixed, wout_ref[...])
    weighted = gain_ref[...] * dot_nt(cot_ref[...].astype(BF), wout_ref[...])
    proj = jnp.mean(weighted * unit, axis=-1, keepdims=True)
    d_gated = inv * (weighted - unit * proj)
    dsc = (d_gated * silu).astype(BF)
    dsc_ref[...] = dsc
    dz_ref[...] = (d_gated * scanned * sig * (1.0 + z * (1.0 - sig))).astype(BF)
    grown = (expand(jnp.exp(base + cum), ee) * dsc.astype(F32)).astype(BF)
    add = dot_tn(cm, grown)

    @pl.when(i == 0)
    def _():
        gst[...] = add

    @pl.when(i > 0)
    def _():
        gst[...] = gst[...] + add

    @pl.when(i == pl.num_programs(0) - 1)
    def _():
        gst_ref[...] = gst[...].astype(BF)


def scan_back_kernel(
    width,
    xc_ref,
    dtv_ref,
    cum_ref,
    base_ref,
    sloc_ref,
    hin_ref,
    gin_ref,
    dsc_ref,
    cin_ref,
    prev_ref,
    cw_ref,
    cb_ref,
    hp_ref,
    skip_ref,
    ee_ref,
    er_ref,
    hot_ref,
    d_ref,
    gconv_ref,
    ghead_ref,
    full_c,
    full_d,
    ds_state,
    kcol,
):
    i = pl.program_id(0)
    n = pl.num_programs(0) - 1
    di = dsc_ref.shape[1]
    cd = cin_ref.shape[1]

    @pl.when(i == 0)
    def _():
        ds_state[...] = gin_ref[...].astype(F32)
        full_d[...] = jnp.zeros_like(full_d)
        kcol[...] = jnp.zeros_like(kcol)
        gconv_ref[...] = jnp.zeros_like(gconv_ref)
        ghead_ref[...] = jnp.zeros_like(ghead_ref)

    @pl.when(i < n)
    def _():
        ee = ee_ref[...]
        xcb = xc_ref[...]
        x = xcb[:, :di].astype(F32)
        bm, cm = xcb[:, di : di + STATE], xcb[:, di + STATE :]
        dtv = dtv_ref[...]
        step = softplus(dtv)
        nega = hp_ref[1:2, :]
        cum = cum_ref[...]
        cum_t = cum.T
        last = cum[Q - 1 : Q, :]
        dyb = dsc_ref[...]
        dy = dyb.astype(F32)
        causal = tri(Q, Q, lambda r, c: c >= r)
        mix_t = jnp.where(causal, dot_nt(bm, cm), 0.0)
        step_e = expand(step, ee)
        u = step_e * x
        ub = u.astype(BF)
        d_mix = jnp.zeros((Q, Q), F32)
        krow = jnp.zeros((Q, LANES), F32)
        du_parts = []
        for p in range(di // (2 * width)):
            cols = slice(2 * width * p, 2 * width * (p + 1))
            dy_blocks = half_blocks(dyb[:, cols], width)
            d_m = dot_nt(ub[:, cols], dy_blocks)
            ms, ks = [], []
            for j in range(2):
                h = 2 * p + j
                fall = jnp.exp(jnp.minimum(cum_t[h : h + 1, :] - cum[:, h : h + 1], 0.0))
                m = mix_t * fall
                d_one = d_m[:, Q * j : Q * (j + 1)]
                d_mix = d_mix + d_one * fall
                kb = (d_one * m).astype(BF)
                kcol[h : h + 1, :] = jnp.sum(kb.astype(F32), axis=0, keepdims=True)
                ms.append(m.astype(BF))
                ks.append(kb)
            du_parts.append(dot(jnp.concatenate(ms, axis=1), dy_blocks))
            krow = krow + dot(jnp.concatenate(ks, axis=1), hot_ref[2 * Q * p : 2 * Q * (p + 1), :])
        dsb = ds_state[...].astype(BF)
        base = base_ref[0:1, :]
        start = sloc_ref[0].astype(F32) + expand_row(jnp.exp(base), ee) * hin_ref[...].astype(F32)
        startb = start.astype(BF)
        tail_e = expand(jnp.exp(last - cum), ee)
        ex = expand(jnp.exp(cum), ee)
        from_state = tail_e * dot(bm, dsb)
        du = jnp.concatenate(du_parts, axis=1) + from_state
        edy = ex * dy
        edyb = edy.astype(BF)
        d_mixb = jnp.where(causal, d_mix, 0.0).astype(BF)
        d_b = dot_nt((tail_e * u).astype(BF), dsb) + dot(d_mixb, cm)
        d_c = dot_nt(edyb, startb) + dot_tn(d_mixb, bm)
        sums = dot(
            jnp.concatenate([edy * dot(cm, startb), u * from_state, x * du], axis=0).astype(BF), er_ref[...]
        )
        rows = jnp.concatenate(
            [
                jnp.sum(start * ds_state[...], axis=0, keepdims=True),
                jnp.sum(dy * x, axis=0, keepdims=True),
                jnp.zeros((6, di), F32),
            ],
            axis=0,
        )
        rows_hi = rows.astype(BF)
        rows_lo = (rows - rows_hi.astype(F32)).astype(BF)
        row_sums = dot(rows_hi, er_ref[...]) + dot(rows_lo, er_ref[...])
        at_end = jnp.exp(last)
        upper = causal.astype(F32)
        strict = tri(Q, Q, lambda r, c: c < r).astype(F32)
        d_decay = (
            dot(upper, kcol[...].T + sums[:Q] - krow, EXACT)
            + dot(strict, sums[Q : 2 * Q], EXACT)
            + at_end * row_sums[0:1]
        )
        d_dt = (sums[2 * Q :] + nega * d_decay) * sigmoid(dtv)
        ghead_ref[0:1, :] += jnp.sum(d_dt, axis=0, keepdims=True)
        ghead_ref[1:2, :] += jnp.sum(d_decay * nega * step, axis=0, keepdims=True)
        ghead_ref[2:3, :] += row_sums[1:2]
        dx = step_e * du + skip_ref[...] * dy
        ds_state[...] = expand_row(at_end, ee) * ds_state[...] + dot_tn(cm, edyb)

        full_c[0:8, :] = prev_ref[HALO - 8 :, :].astype(F32)
        full_c[8:, :] = cin_ref[...].astype(F32)
        summed = cb_ref[...] + cw_ref[0:1, :] * full_c[5 : 5 + Q, :]
        for k in range(1, CONV):
            summed = summed + cw_ref[k : k + 1, :] * full_c[5 + k : 5 + k + Q, :]
        sig = sigmoid(summed)
        slope = sig * (1.0 + summed * (1.0 - sig))
        full_d[0:Q, :di] = dx * slope[:, :di]
        full_d[0:Q, di : di + STATE] = d_b * slope[:, di : di + STATE]
        full_d[0:Q, di + STATE :] = d_c * slope[:, di + STATE :]
        d_sum = full_d[0:Q, :]
        d_cin = cw_ref[CONV - 1 : CONV, :] * d_sum
        for k in range(CONV - 1):
            d_cin = d_cin + cw_ref[k : k + 1, :] * full_d[3 - k : 3 - k + Q, :]
        d_ref[:, :cd] = d_cin.astype(BF)
        d_ref[:, cd:] = d_dt.astype(BF)
        for k in range(CONV):
            gconv_ref[k : k + 1, :] += jnp.sum(d_sum * full_c[5 + k : 5 + k + Q, :], axis=0, keepdims=True)
        gconv_ref[CONV : CONV + 1, :] += jnp.sum(d_sum, axis=0, keepdims=True)
        full_d[Q:, :] = full_d[0:8, :]

    @pl.when(i == n)
    def _():
        full_d[8:16, :] = full_d[Q:, :]
        full_d[0:8, :] = jnp.zeros((8, cd), F32)
        edge = cw_ref[0:1, :] * full_d[3:11, :]
        for k in range(1, CONV):
            edge = edge + cw_ref[k : k + 1, :] * full_d[3 - k : 11 - k, :]
        d_ref[...] = jnp.zeros_like(d_ref)
        d_ref[Q - HALO :, :cd] = jnp.concatenate([jnp.zeros((HALO - 8, cd), F32), edge], axis=0).astype(BF)


def stream_back_kernel(d_ref, dz_ref, wx_ref, wz_ref, gain_ref, s_ref, halo_ref, cot_ref, gs_ref, msg_ref):
    i = pl.program_id(0)

    def through(dn, s):
        inv = root_of(s)
        weighted = gain_ref[...] * dn
        unit = s * inv
        return inv * (weighted - unit * jnp.mean(weighted * unit, axis=-1, keepdims=True))

    @pl.when(i == 0)
    def _():
        msg_ref[...] = through(dot_nt(d_ref[Q - HALO :, :], wx_ref[...]), halo_ref[...])

    @pl.when(i > 0)
    def _():
        dn = dot_nt(d_ref[...], wx_ref[...]) + dot_nt(dz_ref[...], wz_ref[...])
        gs_ref[...] = cot_ref[...] + through(dn, s_ref[...])


def whole(a):
    return pl.BlockSpec(a.shape, lambda *_: (0,) * a.ndim)


def cost(flops, *arrays):
    return pl.CostEstimate(
        flops=int(flops), transcendentals=0, bytes_accessed=sum(a.size * a.dtype.itemsize for a in arrays)
    )


def shape(*dims, dtype=F32):
    return jax.ShapeDtypeStruct(dims, dtype)


def flip(v, axis, n, bit):
    return lax.ppermute(v, axis, [(s, s ^ bit) for s in range(n)])


def shift(v, axis, n, by):
    return lax.ppermute(v, axis, [(s, (s + by) % n) for s in range(n)])


def gather_rows(v, n):
    far = n // 4
    s = lax.axis_index("seq")
    z = s // 4
    buf = jnp.zeros((far,) + v.shape, v.dtype)
    buf = lax.dynamic_update_slice_in_dim(buf, v[None], z, 0)
    for d in range(1, far):
        buf = lax.dynamic_update_slice_in_dim(buf, shift(v, "seq", n, 4 * d)[None], (z - d) % far, 0)
    for bit, axis in ((2, 1), (1, 2)):
        other = flip(buf, "seq", n, bit)
        mine = (s // bit) % 2 == 0
        buf = jnp.where(mine, jnp.stack([buf, other], axis), jnp.stack([other, buf], axis))
    return buf.reshape(n * v.shape[0], v.shape[1])


def scatter_rows(v, n):
    far = n // 4
    s = lax.axis_index("seq")
    z = s // 4
    v = v.reshape(far, 2, 2, v.shape[0] // n, v.shape[1])
    for bit, axis in ((1, 2), (2, 1)):
        me = (s // bit) % 2
        mine = lax.dynamic_index_in_dim(v, me, axis, False)
        other = flip(lax.dynamic_index_in_dim(v, 1 - me, axis, False), "seq", n, bit)
        v = (mine.astype(F32) + other.astype(F32)).astype(BF)
    total = lax.dynamic_index_in_dim(v, z, 0, False).astype(F32)
    for d in range(1, far):
        sent = lax.dynamic_index_in_dim(v, (z + d) % far, 0, False)
        total = total + shift(sent, "seq", n, 4 * d).astype(F32)
    return total


def over_hx(v, hx):
    if hx == 2:
        b = v.astype(BF)
        return b.astype(F32) + flip(b, "hx", hx, 1).astype(F32)
    return lax.psum(v, "hx")


def all_sum(v, n, hx):
    for axis, size in (("seq", n), ("hx", hx)):
        bit = 1
        while bit < size:
            v = v + flip(v, axis, size, bit)
            bit *= 2
    return v


def shards(
    stream,
    cotangent,
    norm_gain,
    in_main,
    in_dt,
    conv_weight,
    conv_bias,
    dt_bias,
    a_log,
    skip_gain,
    gated_gain,
    out_weight,
):
    n, hx = lax.axis_size("seq"), lax.axis_size("hx")
    s, cot = stream[0], cotangent[0]
    t, d = s.shape
    heads = in_dt.shape[1]
    di = out_weight.shape[0] * n
    cd = conv_weight.shape[1] * n
    width = di // heads
    nc = t // Q
    cdp = cd + LANES
    rows = in_main.shape[0]

    halo = lax.ppermute(s[t - HALO :], "hx", [(r, r + 1) for r in range(hx - 1)])
    small = jnp.concatenate([norm_gain, conv_weight.reshape(-1), conv_bias, gated_gain])
    pad = -small.shape[0] % LANES
    small = lax.all_gather(jnp.pad(small, (0, pad))[None], "seq", axis=0, tiled=True)
    cuts = [0]
    for a in (norm_gain, conv_weight, conv_bias, gated_gain):
        cuts.append(cuts[-1] + a.size)
    gain_in = small[:, cuts[0] : cuts[1]].reshape(1, d).astype(F32)
    taps = small[:, cuts[1] : cuts[2]].reshape(n, CONV, cd // n).transpose(1, 0, 2).reshape(CONV, cd).astype(F32)
    taps = jnp.pad(taps, ((0, 8 - CONV), (0, 0)))
    bias = small[:, cuts[2] : cuts[3]].reshape(1, cd).astype(F32)
    gain_gate = small[:, cuts[3] : cuts[4]].reshape(1, di).astype(F32)

    wx = jnp.concatenate([in_main[:, di:], jnp.pad(in_dt, ((0, 0), (0, LANES - heads)))], axis=1)
    wx = gather_rows(wx, n)
    wz = gather_rows(in_main[:, :di], n)
    wo = gather_rows(out_weight, n)

    head_rows = jnp.pad(jnp.stack([dt_bias, -jnp.exp(a_log)]), ((0, 6), (0, LANES - heads)))
    owner = jnp.arange(di, dtype=jnp.int32) // width
    er = (owner[:, None] == jnp.arange(LANES, dtype=jnp.int32)[None, :]).astype(BF)
    one = (jnp.arange(LANES, dtype=jnp.int32)[:, None] == owner[None, :]).astype(BF)
    ee = jnp.concatenate([one, one], axis=0)
    skip = jnp.repeat(skip_gain, width)[None, :]
    hot = (
        (jnp.arange(heads * Q, dtype=jnp.int32) // Q)[:, None] == jnp.arange(LANES, dtype=jnp.int32)[None, :]
    ).astype(BF)

    def at(i):
        return jnp.maximum(i - 1, 0)

    args = (halo, s, gain_in, wx, taps, bias, head_rows, ee)
    nrm, cin, xc, dtv, cum, base, sloc, fin, tot = pl.pallas_call(
        functools.partial(project_kernel, di),
        grid=(nc + 1,),
        in_specs=[whole(halo), pl.BlockSpec((Q, d), lambda i: (at(i), 0))] + [whole(a) for a in args[2:]],
        out_specs=[
            pl.BlockSpec((Q, d), lambda i: (i, 0)),
            pl.BlockSpec((Q, cd), lambda i: (i, 0)),
            pl.BlockSpec((Q, cd), lambda i: (at(i), 0)),
            pl.BlockSpec((Q, LANES), lambda i: (at(i), 0)),
            pl.BlockSpec((Q, LANES), lambda i: (at(i), 0)),
            pl.BlockSpec((8, LANES), lambda i: (at(i), 0)),
            pl.BlockSpec((1, STATE, di), lambda i: (at(i), 0, 0)),
            pl.BlockSpec((STATE, di), lambda i: (0, 0)),
            pl.BlockSpec((8, LANES), lambda i: (0, 0)),
        ],
        out_shape=[
            shape(t + Q, d, dtype=BF),
            shape(t + Q, cd, dtype=BF),
            shape(t, cd, dtype=BF),
            shape(t, LANES),
            shape(t, LANES),
            shape(8 * nc, LANES),
            shape(nc, STATE, di, dtype=BF),
            shape(STATE, di, dtype=BF),
            shape(8, LANES),
        ],
        scratch_shapes=[pltpu.VMEM((Q + 8, cd), F32), pltpu.VMEM((STATE, di), F32), pltpu.VMEM((8, LANES), F32)],
        cost_estimate=cost(3 * t * d * cdp, s, wx, wx, wx),
        name="project",
    )(*args)

    def carry(v, step_by):
        links = [(r, r + step_by) for r in range(hx) if 0 <= r + step_by < hx]
        got = lax.ppermute(v, "hx", links)
        total = got
        if hx > 2:
            fade = jnp.repeat(jnp.exp(tot[0, :heads]), width)[None, :]
            total = got.astype(F32)
            for _ in range(hx - 2):
                got = lax.ppermute((fade * got.astype(F32)).astype(BF), "hx", links)
                total = total + got.astype(F32)
            total = total.astype(BF)
        return total

    hin = carry(fin, 1)

    args = (xc, dtv, cum, nrm, wz, skip, ee)
    yi, gz = pl.pallas_call(
        functools.partial(intra_kernel, width),
        grid=(nc,),
        in_specs=[
            pl.BlockSpec((Q, cd), lambda i: (i, 0)),
            pl.BlockSpec((Q, LANES), lambda i: (i, 0)),
            pl.BlockSpec((Q, LANES), lambda i: (i, 0)),
            pl.BlockSpec((Q, d), lambda i: (i + 1, 0)),
            whole(wz),
            whole(skip),
            whole(ee),
        ],
        out_specs=[pl.BlockSpec((Q, di), lambda i: (i, 0)), pl.BlockSpec((Q, di), lambda i: (i, 0))],
        out_shape=[shape(t, di), shape(t, di)],
        cost_estimate=cost(4 * t * d * di, xc, wz, xc, xc),
        name="intra",
    )(*args)

    args = (yi, gz, xc, cum, base, sloc, hin, s, cot, wo, gain_gate, ee)
    out, mixed, dsc, dz, gst = pl.pallas_call(
        gate_kernel,
        grid=(nc,),
        in_specs=[
            pl.BlockSpec((Q, di), lambda i: (i, 0)),
            pl.BlockSpec((Q, di), lambda i: (i, 0)),
            pl.BlockSpec((Q, cd), lambda i: (i, 0)),
            pl.BlockSpec((Q, LANES), lambda i: (i, 0)),
            pl.BlockSpec((8, LANES), lambda i: (i, 0)),
            pl.BlockSpec((1, STATE, di), lambda i: (i, 0, 0)),
            whole(hin),
            pl.BlockSpec((Q, d), lambda i: (i, 0)),
            pl.BlockSpec((Q, d), lambda i: (i, 0)),
            whole(wo),
            whole(gain_gate),
            whole(ee),
        ],
        out_specs=[
            pl.BlockSpec((Q, d), lambda i: (i, 0)),
            pl.BlockSpec((Q, di), lambda i: (i, 0)),
            pl.BlockSpec((Q, di), lambda i: (i, 0)),
            pl.BlockSpec((Q, di), lambda i: (i, 0)),
            pl.BlockSpec((STATE, di), lambda i: (0, 0)),
        ],
        out_shape=[
            shape(t, d),
            shape(t, di, dtype=BF),
            shape(t, di, dtype=BF),
            shape(t, di, dtype=BF),
            shape(STATE, di, dtype=BF),
        ],
        scratch_shapes=[pltpu.VMEM((STATE, di), F32)],
        cost_estimate=cost(6 * t * d * di, yi, gz, xc, s, s, s),
        name="gate",
    )(*args)

    gin = carry(gst, -1)
    g_out = dot_tn(mixed, cot.astype(BF)).astype(BF)
    g_z = dot_tn(nrm[Q:], dz).astype(BF)

    args = (xc, dtv, cum, base, sloc, hin, gin, dsc, cin, cin, taps, bias, head_rows, skip, ee, er, hot)

    def back(i):
        return jnp.maximum(nc - 1 - i, 0)

    per = Q // HALO
    dx, gconv, ghead = pl.pallas_call(
        functools.partial(scan_back_kernel, width),
        grid=(nc + 1,),
        in_specs=[
            pl.BlockSpec((Q, cd), lambda i: (back(i), 0)),
            pl.BlockSpec((Q, LANES), lambda i: (back(i), 0)),
            pl.BlockSpec((Q, LANES), lambda i: (back(i), 0)),
            pl.BlockSpec((8, LANES), lambda i: (back(i), 0)),
            pl.BlockSpec((1, STATE, di), lambda i: (back(i), 0, 0)),
            whole(hin),
            whole(gin),
            pl.BlockSpec((Q, di), lambda i: (back(i), 0)),
            pl.BlockSpec((Q, cd), lambda i: (back(i) + 1, 0)),
            pl.BlockSpec((HALO, cd), lambda i: ((back(i) + 1) * per - 1, 0)),
        ]
        + [whole(a) for a in args[10:]],
        out_specs=[
            pl.BlockSpec((Q, cdp), lambda i: (nc - i, 0)),
            pl.BlockSpec((8, cd), lambda i: (0, 0)),
            pl.BlockSpec((8, LANES), lambda i: (0, 0)),
        ],
        out_shape=[shape(t + Q, cdp, dtype=BF), shape(8, cd), shape(8, LANES)],
        scratch_shapes=[
            pltpu.VMEM((Q + 8, cd), F32),
            pltpu.VMEM((Q + 8, cd), F32),
            pltpu.VMEM((STATE, di), F32),
            pltpu.VMEM((LANES, Q), F32),
        ],
        cost_estimate=cost(8 * t * d * di, xc, xc, xc, xc),
        name="scan_back",
    )(*args)

    g_x = dot_tn(nrm, dx).astype(BF)

    args = (dx, dz, wx, wz, gain_in, s, halo, cot)
    g_stream, msg = pl.pallas_call(
        stream_back_kernel,
        grid=(nc + 1,),
        in_specs=[
            pl.BlockSpec((Q, cdp), lambda i: (i, 0)),
            pl.BlockSpec((Q, di), lambda i: (at(i), 0)),
            whole(wx),
            whole(wz),
            whole(gain_in),
            pl.BlockSpec((Q, d), lambda i: (at(i), 0)),
            whole(halo),
            pl.BlockSpec((Q, d), lambda i: (at(i), 0)),
        ],
        out_specs=[pl.BlockSpec((Q, d), lambda i: (at(i), 0)), pl.BlockSpec((HALO, d), lambda i: (0, 0))],
        out_shape=[shape(t, d), shape(HALO, d)],
        cost_estimate=cost(2 * t * d * (di + cdp), s, s, s, wx, wz),
        name="stream_back",
    )(*args)
    msg = lax.ppermute(msg, "hx", [(r + 1, r) for r in range(hx - 1)])
    g_stream = lax.dynamic_update_slice(g_stream, g_stream[t - HALO :] + msg, (t - HALO, 0))

    packed = jnp.concatenate([gconv, jnp.pad(ghead, ((0, 0), (0, 2 * LANES - ghead.shape[1])))], axis=1)
    packed = all_sum(packed, n, hx)
    mine = lax.dynamic_slice_in_dim(packed[:, :cd], lax.axis_index("seq") * (cd // n), cd // n, 1)

    g_out = over_hx(scatter_rows(g_out, n), hx)
    g_z = over_hx(scatter_rows(g_z, n), hx)
    g_x = over_hx(scatter_rows(g_x, n), hx)
    g_main = jnp.concatenate([g_z, g_x[:, : cd]], axis=1)
    g_dt = g_x[:, cd : cd + heads]
    g_norm = (
        jnp.sum(in_main.astype(F32) * g_main, axis=1) + jnp.sum(in_dt.astype(F32) * g_dt, axis=1)
    ) / norm_gain.astype(F32)
    g_gate = jnp.sum(out_weight.astype(F32) * g_out, axis=1) / gated_gain.astype(F32)
    return (
        out[None],
        g_stream[None],
        g_norm,
        g_main,
        g_dt,
        mine[:CONV],
        mine[CONV],
        packed[0, cd : cd + heads],
        packed[1, cd : cd + heads],
        packed[2, cd : cd + heads],
        g_gate,
        g_out,
    )


def solution(mesh):
    placed = (
        P("seq", "hx", None),
        P("seq", "hx", None),
        P("seq"),
        P("seq", None),
        P("seq", None),
        P(None, "seq"),
        P("seq"),
        P(),
        P(),
        P(),
        P("seq"),
        P("seq", None),
    )
    return jax.shard_map(
        shards,
        mesh=mesh,
        in_specs=placed,
        out_specs=(
            P("seq", "hx", None),
            P("seq", "hx", None),
            P("seq"),
            P("seq", None),
            P("seq", None),
            P(None, "seq"),
            P("seq"),
            P(),
            P(),
            P(),
            P("seq"),
            P("seq", None),
        ),
        check_vma=False,
    )
```

```python
import functools

import jax
import jax.numpy as jnp
from jax import lax
from jax.experimental import pallas as pl
from jax.experimental.pallas import tpu as pltpu
from jax.sharding import PartitionSpec as P

STATE = 128
CONV = 4
EPSILON = 1e-05
Q = 128
LANES = 128
GROUP = 256
HALO = 16
BF = jnp.bfloat16
F32 = jnp.float32
EXACT = lax.Precision.HIGHEST


def dot(a, b, precision=None):
    return lax.dot_general(
        a, b, (((1,), (0,)), ((), ())), precision=precision, preferred_element_type=F32
    )


def dot_nt(a, b):
    return lax.dot_general(a, b, (((1,), (1,)), ((), ())), preferred_element_type=F32)


def dot_tn(a, b):
    return lax.dot_general(a, b, (((0,), (0,)), ((), ())), preferred_element_type=F32)


def two_terms(v):
    hi = v.astype(BF)
    lo = (v - hi.astype(F32)).astype(BF)
    return jnp.concatenate([hi, lo], axis=1)


def expand(v, ee):
    return dot(two_terms(v), ee)


def expand_row(v, ee):
    return expand(jnp.broadcast_to(v, (8, v.shape[1])), ee)[0:1]


def softplus(v):
    return jnp.maximum(v, 0.0) + jnp.log1p(jnp.exp(-jnp.abs(v)))


def sigmoid(v):
    return 1.0 / (1.0 + jnp.exp(-v))


def root_of(v):
    return lax.rsqrt(jnp.mean(v * v, axis=-1, keepdims=True) + EPSILON)


def tri(rows, cols, keep):
    r = lax.broadcasted_iota(jnp.int32, (rows, cols), 0)
    c = lax.broadcasted_iota(jnp.int32, (rows, cols), 1)
    return keep(r, c)


def half_blocks(v, width):
    lane = lax.broadcasted_iota(jnp.int32, v.shape, 1)
    zero = jnp.zeros_like(v)
    return jnp.concatenate([jnp.where(lane < width, v, zero), jnp.where(lane >= width, v, zero)], axis=0)


def project_kernel(
    n,
    halo_ref,
    s_ref,
    wa_ref,
    wb_ref,
    hp_ref,
    ee_ref,
    nrm_ref,
    cin_ref,
    xc_ref,
    slope_ref,
    dtv_ref,
    cum_ref,
    base_ref,
    sloc_ref,
    fin_ref,
    tot_ref,
    small_ref,
    full,
    state,
    base,
):
    i = pl.program_id(0)
    cd = cin_ref.shape[1]
    di = fin_ref.shape[1]
    d, ca = wa_ref.shape
    rows = d // n

    def columns(lo, hi):
        if hi <= ca:
            return wa_ref[:, lo:hi]
        return wb_ref[:, lo - ca : hi - ca]

    @pl.when(i == 0)
    def _():
        small_ref[...] = jnp.zeros_like(small_ref)
        for k in range(n):
            piece = wb_ref[rows * k : rows * k + 8, cd + LANES - ca :].astype(F32)
            for row, size in ((0, d // n), (6, di // n)):
                small_ref[row : row + 1, size * k : size * (k + 1)] = piece[row : row + 1, :size]
            size = cd // n
            small_ref[1:6, size * k : size * (k + 1)] = piece[1:6, :size]
        h = halo_ref[...]
        nh = (h * root_of(h) * small_ref[0:1, :d]).astype(BF)
        nrm_ref[...] = jnp.zeros_like(nrm_ref)
        nrm_ref[Q - HALO :, :] = nh
        cin_ref[...] = jnp.zeros_like(cin_ref)
        ph = jnp.concatenate([dot(nh, columns(0, ca)), dot(nh, columns(ca, cd))], axis=1).astype(BF)
        cin_ref[Q - HALO :, :] = ph
        full[0:8, :] = ph.astype(F32)[HALO - 8 :]
        state[...] = jnp.zeros_like(state)
        base[...] = jnp.zeros_like(base)

    @pl.when(i > 0)
    def _():
        s = s_ref[...]
        nrm = (s * root_of(s) * small_ref[0:1, :d]).astype(BF)
        nrm_ref[...] = nrm
        dtv = dot(nrm, columns(cd, cd + LANES)).astype(BF).astype(F32) + hp_ref[0:1, :]
        dtv_ref[...] = dtv
        step = softplus(dtv)
        lower = tri(Q, Q, lambda r, c: r >= c).astype(F32)
        cum = dot(lower, hp_ref[1:2, :] * step, EXACT)
        cum_ref[...] = cum
        last = cum[Q - 1 : Q, :]
        base_ref[...] = base[...]
        base[...] = base[...] + last
        weight = two_terms(jnp.exp(last - cum) * step)
        at_end = two_terms(jnp.broadcast_to(jnp.exp(last), (8, LANES)))

        def conv(lo, hi):
            cin = dot(nrm, columns(lo, hi)).astype(BF)
            cin_ref[:, lo:hi] = cin
            full[8:, lo:hi] = cin.astype(F32)
            summed = small_ref[5:6, lo:hi] + small_ref[4:5, lo:hi] * full[8:, lo:hi]
            for k in range(CONV - 1):
                summed = summed + small_ref[k + 1 : k + 2, lo:hi] * full[5 + k : 5 + k + Q, lo:hi]
            full[0:8, lo:hi] = full[Q : Q + 8, lo:hi]
            sig = sigmoid(summed)
            xc = summed * sig
            slope_ref[:, lo:hi] = (sig + xc * (1.0 - sig)).astype(BF)
            xcb = xc.astype(BF)
            xc_ref[:, lo:hi] = xcb
            return xc, xcb

        _, bc = conv(di, cd)
        bm = bc[:, :STATE]
        for lo in range(0, di, GROUP):
            cols = slice(lo, lo + GROUP)
            xc, _ = conv(lo, lo + GROUP)
            sloc_ref[0, :, cols] = state[:, cols].astype(BF)
            u = (dot(weight, ee_ref[:, cols]) * xc).astype(BF)
            state[:, cols] = state[:, cols] * dot(at_end, ee_ref[:, cols])[0:1] + dot_tn(bm, u)

    @pl.when(i == pl.num_programs(0) - 1)
    def _():
        fin_ref[...] = state[...].astype(BF)
        tot_ref[...] = base[...]


def intra_kernel(width, xc_ref, dtv_ref, cum_ref, skip_ref, ee_ref, yi_ref):
    di = yi_ref.shape[1]
    bm, cm = xc_ref[:, di : di + STATE], xc_ref[:, di + STATE :]
    cum = cum_ref[...]
    cum_t = cum.T
    mix = jnp.where(tri(Q, Q, lambda r, c: r >= c), dot_nt(cm, bm), 0.0)
    step = two_terms(softplus(dtv_ref[...]))
    for lo in range(0, di, GROUP):
        cols = slice(lo, lo + GROUP)
        x = xc_ref[:, cols].astype(F32)
        ub = (dot(step, ee_ref[:, cols]) * x).astype(BF)
        parts = []
        for q in range(0, GROUP, 2 * width):
            two = []
            for h in ((lo + q) // width, (lo + q) // width + 1):
                gap = jnp.minimum(cum[:, h : h + 1] - cum_t[h : h + 1, :], 0.0)
                two.append((jnp.exp(gap) * mix).astype(BF))
            parts.append(dot(jnp.concatenate(two, axis=1), half_blocks(ub[:, q : q + 2 * width], width)))
        yi_ref[:, cols] = (jnp.concatenate(parts, axis=1) + skip_ref[:, cols] * x).astype(BF)


def gate_kernel(
    n,
    yi_ref,
    nrm_ref,
    c_ref,
    cum_ref,
    base_ref,
    sloc_ref,
    hin_ref,
    s_ref,
    cot_ref,
    wzo_ref,
    small_ref,
    ee_ref,
    out_ref,
    mixed_ref,
    dsc_ref,
    dz_ref,
    gst_ref,
    gst,
    wo,
):
    i = pl.program_id(0)
    di = yi_ref.shape[1]
    d = s_ref.shape[1]

    @pl.when(i == 0)
    def _():
        rows, per = d // n, di // d
        for k in range(n):
            for a in range(per):
                at = (per * k + a) * rows
                wo[at : at + rows, :] = wzo_ref[rows * k : rows * (k + 1), di + d * a : di + d * (a + 1)]

    ee = ee_ref[...]
    cm = c_ref[...]
    cum = cum_ref[...]
    base = base_ref[0:1, :]
    start = (sloc_ref[0].astype(F32) + expand_row(jnp.exp(base), ee) * hin_ref[...].astype(F32)).astype(BF)
    ex = expand(jnp.exp(cum), ee)
    scanned = (yi_ref[...].astype(F32) + ex * dot(cm, start)).astype(BF).astype(F32)
    z = dot(nrm_ref[...], wzo_ref[:, :di])
    sig = sigmoid(z)
    silu = z * sig
    gated = scanned * silu
    inv = root_of(gated)
    unit = gated * inv
    gain = small_ref[6:7, :di]
    mixed = (unit * gain).astype(BF)
    mixed_ref[...] = mixed
    out_ref[...] = s_ref[...] + dot(mixed, wo[...])
    weighted = gain * dot_nt(cot_ref[...].astype(BF), wo[...])
    proj = jnp.mean(weighted * unit, axis=-1, keepdims=True)
    d_gated = inv * (weighted - unit * proj)
    dsc = (d_gated * silu).astype(BF)
    dsc_ref[...] = dsc
    dz_ref[...] = (d_gated * scanned * (sig + silu * (1.0 - sig))).astype(BF)
    grown = (expand(jnp.exp(base + cum), ee) * dsc.astype(F32)).astype(BF)
    add = dot_tn(cm, grown)

    @pl.when(i == 0)
    def _():
        gst[...] = add

    @pl.when(i > 0)
    def _():
        gst[...] = gst[...] + add

    @pl.when(i == pl.num_programs(0) - 1)
    def _():
        gst_ref[...] = gst[...].astype(BF)


def scan_back_kernel(
    width,
    xc_ref,
    slope_ref,
    dtv_ref,
    cum_ref,
    base_ref,
    sloc_ref,
    hin_ref,
    gin_ref,
    dsc_ref,
    cin_ref,
    prev_ref,
    small_ref,
    hp_ref,
    skip_ref,
    ee_ref,
    er_ref,
    hot_ref,
    d_ref,
    gconv_ref,
    ghead_ref,
    full_d,
    ds_state,
    kcol,
):
    i = pl.program_id(0)
    n = pl.num_programs(0) - 1
    di = dsc_ref.shape[1]
    cd = cin_ref.shape[1]

    def tap(k, cols=slice(None)):
        return small_ref[k + 1 : k + 2, cols]

    @pl.when(i == 0)
    def _():
        ds_state[...] = gin_ref[...].astype(F32)
        full_d[...] = jnp.zeros_like(full_d)
        kcol[...] = jnp.zeros_like(kcol)
        gconv_ref[...] = jnp.zeros_like(gconv_ref)
        ghead_ref[...] = jnp.zeros_like(ghead_ref)

    @pl.when(i < n)
    def _():
        bm, cm = xc_ref[:, di : di + STATE], xc_ref[:, di + STATE :]
        dtv = dtv_ref[...]
        step = softplus(dtv)
        nega = hp_ref[1:2, :]
        cum = cum_ref[...]
        cum_t = cum.T
        last = cum[Q - 1 : Q, :]
        causal = tri(Q, Q, lambda r, c: c >= r)
        mix_t = jnp.where(causal, dot_nt(bm, cm), 0.0)
        step_2 = two_terms(step)
        tail_2 = two_terms(jnp.exp(last - cum))
        ex_2 = two_terms(jnp.exp(cum))
        at_end = jnp.exp(last)
        rows_2 = two_terms(jnp.concatenate([jnp.exp(base_ref[0:1, :]), at_end, jnp.zeros((6, LANES), F32)], axis=0))
        d_mix = jnp.zeros((Q, Q), F32)
        krow = jnp.zeros((Q, LANES), F32)
        d_b, d_c = jnp.zeros((Q, STATE), F32), jnp.zeros((Q, STATE), F32)
        sums = jnp.zeros((3 * Q, LANES), F32)
        row_sums = jnp.zeros((16, LANES), F32)

        def conv_back(cols, d_sum):
            full_d[0:Q, cols] = d_sum
            cin = cin_ref[:, cols].astype(F32)
            d_cin = tap(CONV - 1, cols) * d_sum
            gconv_ref[CONV - 1 : CONV, cols] += jnp.sum(d_sum * cin, axis=0, keepdims=True)
            gconv_ref[CONV : CONV + 1, cols] += jnp.sum(d_sum, axis=0, keepdims=True)
            for k in range(CONV - 1):
                later = full_d[3 - k : 3 - k + Q, cols]
                d_cin = d_cin + tap(k, cols) * later
                gconv_ref[k : k + 1, cols] += jnp.sum(later * cin, axis=0, keepdims=True)
            d_ref[:, cols] = d_cin.astype(BF)
            full_d[Q:, cols] = full_d[0:8, cols]

        for lo in range(0, di, GROUP):
            cols = slice(lo, lo + GROUP)
            ee = ee_ref[:, cols]
            x = xc_ref[:, cols].astype(F32)
            dyb = dsc_ref[:, cols]
            dy = dyb.astype(F32)
            step_e = dot(step_2, ee)
            u = step_e * x
            ub = u.astype(BF)
            parts = []
            for q in range(0, GROUP, 2 * width):
                pair = slice(q, q + 2 * width)
                dy_blocks = half_blocks(dyb[:, pair], width)
                d_m = dot_nt(ub[:, pair], dy_blocks)
                ms, ks = [], []
                first = (lo + q) // width
                for j in range(2):
                    h = first + j
                    fall = jnp.exp(jnp.minimum(cum_t[h : h + 1, :] - cum[:, h : h + 1], 0.0))
                    m = mix_t * fall
                    d_one = d_m[:, Q * j : Q * (j + 1)]
                    d_mix = d_mix + d_one * fall
                    kb = (d_one * m).astype(BF)
                    kcol[h : h + 1, :] = jnp.sum(kb.astype(F32), axis=0, keepdims=True)
                    ms.append(m.astype(BF))
                    ks.append(kb)
                parts.append(dot(jnp.concatenate(ms, axis=1), dy_blocks))
                krow = krow + dot(jnp.concatenate(ks, axis=1), hot_ref[Q * first : Q * (first + 2), :])
            d_state = ds_state[:, cols]
            dsb = d_state.astype(BF)
            rows_e = dot(rows_2, ee)
            start = sloc_ref[0, :, cols].astype(F32) + rows_e[0:1] * hin_ref[:, cols].astype(F32)
            startb = start.astype(BF)
            tail_e = dot(tail_2, ee)
            from_state = tail_e * dot(bm, dsb)
            du = jnp.concatenate(parts, axis=1) + from_state
            edy = dot(ex_2, ee) * dy
            edyb = edy.astype(BF)
            d_b = d_b + dot_nt((tail_e * u).astype(BF), dsb)
            d_c = d_c + dot_nt(edyb, startb)
            three = jnp.concatenate([edy * dot(cm, startb), u * from_state, x * du], axis=0).astype(BF)
            sums = sums + dot(three, er_ref[cols, :])
            rows = jnp.concatenate(
                [
                    jnp.sum(start * d_state, axis=0, keepdims=True),
                    jnp.sum(dy * x, axis=0, keepdims=True),
                    jnp.zeros((6, GROUP), F32),
                ],
                axis=0,
            )
            rows_hi = rows.astype(BF)
            rows_lo = (rows - rows_hi.astype(F32)).astype(BF)
            row_sums = row_sums + dot(jnp.concatenate([rows_hi, rows_lo], axis=0), er_ref[cols, :])
            ds_state[:, cols] = rows_e[1:2] * d_state + dot_tn(cm, edyb)
            conv_back(cols, (step_e * du + skip_ref[:, cols] * dy) * slope_ref[:, cols].astype(F32))

        d_mixb = jnp.where(causal, d_mix, 0.0).astype(BF)
        d_bc = jnp.concatenate([d_b + dot(d_mixb, cm), d_c + dot_tn(d_mixb, bm)], axis=1)
        conv_back(slice(di, cd), d_bc * slope_ref[:, di:].astype(F32))
        upper = causal.astype(F32)
        strict = tri(Q, Q, lambda r, c: c < r).astype(F32)
        row_sums = row_sums[0:8] + row_sums[8:16]
        d_decay = (
            dot(upper, kcol[...].T + sums[:Q] - krow, EXACT)
            + dot(strict, sums[Q : 2 * Q], EXACT)
            + at_end * row_sums[0:1]
        )
        d_dt = (sums[2 * Q :] + nega * d_decay) * sigmoid(dtv)
        d_ref[:, cd:] = d_dt.astype(BF)
        ghead_ref[0:1, :] += jnp.sum(d_dt, axis=0, keepdims=True)
        ghead_ref[1:2, :] += jnp.sum(d_decay * nega * step, axis=0, keepdims=True)
        ghead_ref[2:3, :] += row_sums[1:2]

    @pl.when(i == n)
    def _():
        full_d[8:16, :] = full_d[Q:, :]
        full_d[0:8, :] = jnp.zeros((8, cd), F32)
        cin = prev_ref[HALO - 8 :, :].astype(F32)
        edge = jnp.zeros((8, cd), F32)
        for k in range(CONV - 1):
            later = full_d[3 - k : 11 - k, :]
            edge = edge + tap(k) * later
            gconv_ref[k : k + 1, :] += jnp.sum(later * cin, axis=0, keepdims=True)
        d_ref[...] = jnp.zeros_like(d_ref)
        d_ref[Q - HALO :, :cd] = jnp.concatenate([jnp.zeros((HALO - 8, cd), F32), edge], axis=0).astype(BF)


def stream_back_kernel(d_ref, dnz_ref, wa_ref, wb_ref, small_ref, s_ref, halo_ref, cot_ref, gs_ref, msg_ref):
    i = pl.program_id(0)
    d, ca = wa_ref.shape
    cdp = d_ref.shape[1]

    def through(dn, s):
        inv = root_of(s)
        weighted = small_ref[0:1, :d] * dn
        unit = s * inv
        return inv * (weighted - unit * jnp.mean(weighted * unit, axis=-1, keepdims=True))

    def back(rows):
        return dot_nt(rows[:, :ca], wa_ref[...]) + dot_nt(rows[:, ca:], wb_ref[:, : cdp - ca])

    @pl.when(i == 0)
    def _():
        msg_ref[...] = through(back(d_ref[Q - HALO :, :]), halo_ref[...])

    @pl.when(i > 0)
    def _():
        gs_ref[...] = cot_ref[...] + through(dnz_ref[...] + back(d_ref[...]), s_ref[...])


VMEM = pltpu.CompilerParams(vmem_limit_bytes=60 * 2**20)


def whole(a):
    return pl.BlockSpec(a.shape, lambda *_: (0,) * a.ndim)


def cost(flops, *arrays):
    return pl.CostEstimate(
        flops=int(flops), transcendentals=0, bytes_accessed=sum(a.size * a.dtype.itemsize for a in arrays)
    )


def shape(*dims, dtype=F32):
    return jax.ShapeDtypeStruct(dims, dtype)


def flip(v, axis, n, bit):
    return lax.ppermute(v, axis, [(s, s ^ bit) for s in range(n)])


def shift(v, axis, n, by):
    return lax.ppermute(v, axis, [(s, (s + by) % n) for s in range(n)])


def far_gather(v, n):
    far = n // 4
    z = lax.axis_index("seq") // 4
    got = [v] + [shift(v, "seq", n, 4 * k) for k in range(1, far)]
    buf = jnp.zeros((far,) + v.shape, v.dtype)
    for k in range(far):
        buf = lax.dynamic_update_slice_in_dim(buf, got[k][None], (z - k) % far, 0)
    return buf


def pair_gather(v, n, bit, axis):
    other = flip(v, "seq", n, bit)
    mine = (lax.axis_index("seq") // bit) % 2 == 0
    return jnp.where(mine, jnp.stack([v, other], axis), jnp.stack([other, v], axis))


def gather_rows(v, n, ca):
    a, b = v[:, :ca], v[:, ca:]
    b = pair_gather(b, n, 2, 0)
    a = far_gather(a, n)
    a = pair_gather(a, n, 2, 1)
    b = far_gather(b, n)
    a, b = pair_gather(a, n, 1, 2), pair_gather(b, n, 1, 2)
    return a.reshape(-1, a.shape[-1]), b.reshape(-1, b.shape[-1])


def pair_scatter(v, n, bit, axis):
    me = (lax.axis_index("seq") // bit) % 2
    mine = lax.dynamic_index_in_dim(v, me, axis, False)
    other = flip(lax.dynamic_index_in_dim(v, 1 - me, axis, False), "seq", n, bit)
    return (mine.astype(F32) + other.astype(F32)).astype(BF)


def far_scatter(v, n):
    far = n // 4
    z = lax.axis_index("seq") // 4
    total = lax.dynamic_index_in_dim(v, z, 0, False).astype(F32)
    for k in range(1, far):
        sent = lax.dynamic_index_in_dim(v, (z + k) % far, 0, False)
        total = total + shift(sent, "seq", n, 4 * k).astype(F32)
    return total.astype(BF)


def scatter_rows(v, n, ca):
    v = v.reshape(n // 4, 2, 2, v.shape[0] // n, v.shape[1])
    v = pair_scatter(v, n, 1, 2)
    a, b = v[..., :ca], v[..., ca:]
    a = pair_scatter(a, n, 2, 1)
    b = far_scatter(b, n)
    a = far_scatter(a, n)
    b = pair_scatter(b, n, 2, 0)
    return jnp.concatenate([a, b], axis=-1)


def over_hx(v, hx):
    if hx == 2:
        b = v.astype(BF)
        return b.astype(F32) + flip(b, "hx", hx, 1).astype(F32)
    return lax.psum(v.astype(F32), "hx")


def all_sum(v, n, hx):
    for axis, size in (("seq", n), ("hx", hx)):
        bit = 1
        while bit < size:
            v = v + flip(v, axis, size, bit)
            bit *= 2
    return v


def shards(
    stream,
    cotangent,
    norm_gain,
    in_main,
    in_dt,
    conv_weight,
    conv_bias,
    dt_bias,
    a_log,
    skip_gain,
    gated_gain,
    out_weight,
):
    n, hx = lax.axis_size("seq"), lax.axis_size("hx")
    s, cot = stream[0], cotangent[0]
    t, d = s.shape
    heads = in_dt.shape[1]
    di = out_weight.shape[0] * n
    cd = conv_weight.shape[1] * n
    width = di // heads
    nc = t // Q
    cdp = cd + LANES
    rows = in_main.shape[0]
    per = di // d

    def lanes(v):
        return jnp.pad(v, ((0, 0), (0, LANES - v.shape[1])))

    small = jnp.concatenate(
        [lanes(norm_gain[None]), lanes(conv_weight), lanes(conv_bias[None]), lanes(gated_gain[None])], axis=0
    )
    small = jnp.pad(small, ((0, rows - small.shape[0]), (0, 0)))
    wx = jnp.concatenate([in_main[:, di:], lanes(in_dt), small], axis=1)
    ca = wx.shape[1] * 2 // 3 // GROUP * GROUP
    wa, wb = gather_rows(wx, n, ca)
    wzo = jnp.concatenate([in_main[:, :di], out_weight.reshape(per, rows, d).transpose(1, 0, 2).reshape(rows, di)], axis=1)
    wzo = lax.all_gather(wzo, "seq", axis=0, tiled=True)
    halo = lax.ppermute(s[t - HALO :], "hx", [(r, r + 1) for r in range(hx - 1)])

    head_rows = jnp.pad(jnp.stack([dt_bias, -jnp.exp(a_log)]), ((0, 6), (0, LANES - heads)))
    owner = jnp.arange(di, dtype=jnp.int32) // width
    er = (owner[:, None] == jnp.arange(LANES, dtype=jnp.int32)[None, :]).astype(BF)
    one = (jnp.arange(LANES, dtype=jnp.int32)[:, None] == owner[None, :]).astype(BF)
    ee = jnp.concatenate([one, one], axis=0)
    skip = jnp.repeat(skip_gain, width)[None, :]
    hot = (
        (jnp.arange(heads * Q, dtype=jnp.int32) // Q)[:, None] == jnp.arange(LANES, dtype=jnp.int32)[None, :]
    ).astype(BF)

    def at(i):
        return jnp.maximum(i - 1, 0)

    args = (halo, s, wa, wb, head_rows, ee)
    nrm, cin, xc, slope, dtv, cum, base, sloc, fin, tot, small = pl.pallas_call(
        functools.partial(project_kernel, n),
        grid=(nc + 1,),
        in_specs=[whole(halo), pl.BlockSpec((Q, d), lambda i: (at(i), 0))] + [whole(a) for a in args[2:]],
        out_specs=[
            pl.BlockSpec((Q, d), lambda i: (i, 0)),
            pl.BlockSpec((Q, cd), lambda i: (i, 0)),
            pl.BlockSpec((Q, cd), lambda i: (at(i), 0)),
            pl.BlockSpec((Q, cd), lambda i: (at(i), 0)),
            pl.BlockSpec((Q, LANES), lambda i: (at(i), 0)),
            pl.BlockSpec((Q, LANES), lambda i: (at(i), 0)),
            pl.BlockSpec((8, LANES), lambda i: (at(i), 0)),
            pl.BlockSpec((1, STATE, di), lambda i: (at(i), 0, 0)),
            pl.BlockSpec((STATE, di), lambda i: (0, 0)),
            pl.BlockSpec((8, LANES), lambda i: (0, 0)),
            pl.BlockSpec((8, cd), lambda i: (0, 0)),
        ],
        out_shape=[
            shape(t + Q, d, dtype=BF),
            shape(t + Q, cd, dtype=BF),
            shape(t, cd, dtype=BF),
            shape(t, cd, dtype=BF),
            shape(t, LANES),
            shape(t, LANES),
            shape(8 * nc, LANES),
            shape(nc, STATE, di, dtype=BF),
            shape(STATE, di, dtype=BF),
            shape(8, LANES),
            shape(8, cd),
        ],
        scratch_shapes=[pltpu.VMEM((Q + 8, cd), F32), pltpu.VMEM((STATE, di), F32), pltpu.VMEM((8, LANES), F32)],
        compiler_params=VMEM,
        cost_estimate=cost(3 * t * d * cdp, s, wa, wb, s, s),
        name="project",
    )(*args)

    def carry(v, step_by):
        links = [(r, r + step_by) for r in range(hx) if 0 <= r + step_by < hx]
        got = lax.ppermute(v, "hx", links)
        total = got
        if hx > 2:
            fade = jnp.repeat(jnp.exp(tot[0, :heads]), width)[None, :]
            total = got.astype(F32)
            for _ in range(hx - 2):
                got = lax.ppermute((fade * got.astype(F32)).astype(BF), "hx", links)
                total = total + got.astype(F32)
            total = total.astype(BF)
        return total

    hin = carry(fin, 1)

    args = (xc, dtv, cum, skip, ee)
    yi = pl.pallas_call(
        functools.partial(intra_kernel, width),
        grid=(nc,),
        in_specs=[
            pl.BlockSpec((Q, cd), lambda i: (i, 0)),
            pl.BlockSpec((Q, LANES), lambda i: (i, 0)),
            pl.BlockSpec((Q, LANES), lambda i: (i, 0)),
            whole(skip),
            whole(ee),
        ],
        out_specs=pl.BlockSpec((Q, di), lambda i: (i, 0)),
        out_shape=shape(t, di, dtype=BF),
        compiler_params=VMEM,
        cost_estimate=cost(2 * t * d * di, xc, xc),
        name="intra",
    )(*args)

    args = (yi, nrm, xc, cum, base, sloc, hin, s, cot, wzo, small, ee)
    out, mixed, dsc, dz, gst = pl.pallas_call(
        functools.partial(gate_kernel, n),
        grid=(nc,),
        in_specs=[
            pl.BlockSpec((Q, di), lambda i: (i, 0)),
            pl.BlockSpec((Q, d), lambda i: (i + 1, 0)),
            pl.BlockSpec((Q, STATE), lambda i: (i, cd // STATE - 1)),
            pl.BlockSpec((Q, LANES), lambda i: (i, 0)),
            pl.BlockSpec((8, LANES), lambda i: (i, 0)),
            pl.BlockSpec((1, STATE, di), lambda i: (i, 0, 0)),
            whole(hin),
            pl.BlockSpec((Q, d), lambda i: (i, 0)),
            pl.BlockSpec((Q, d), lambda i: (i, 0)),
            whole(wzo),
            whole(small),
            whole(ee),
        ],
        out_specs=[
            pl.BlockSpec((Q, d), lambda i: (i, 0)),
            pl.BlockSpec((Q, di), lambda i: (i, 0)),
            pl.BlockSpec((Q, di), lambda i: (i, 0)),
            pl.BlockSpec((Q, di), lambda i: (i, 0)),
            pl.BlockSpec((STATE, di), lambda i: (0, 0)),
        ],
        out_shape=[
            shape(t, d),
            shape(t, di, dtype=BF),
            shape(t, di, dtype=BF),
            shape(t, di, dtype=BF),
            shape(STATE, di, dtype=BF),
        ],
        scratch_shapes=[pltpu.VMEM((STATE, di), F32), pltpu.VMEM((di, d), BF)],
        compiler_params=VMEM,
        cost_estimate=cost(6 * t * d * di, yi, yi, yi, xc, s, s, s),
        name="gate",
    )(*args)

    gin = carry(gst, -1)
    g_z = dot_tn(nrm[Q:], dz).astype(BF)
    g_out = dot_tn(mixed, cot.astype(BF)).astype(BF)
    g_zo = jnp.concatenate([g_z, g_out.reshape(n, per, rows, d).transpose(0, 2, 1, 3).reshape(d, di)], axis=1)
    g_zo = lax.psum_scatter(g_zo, "seq", scatter_dimension=0, tiled=True)
    dnz = dot_nt(dz, wzo[:, :di])

    args = (xc, slope, dtv, cum, base, sloc, hin, gin, dsc, cin, cin, small, head_rows, skip, ee, er, hot)

    def back(i):
        return jnp.maximum(nc - 1 - i, 0)

    dx, gconv, ghead = pl.pallas_call(
        functools.partial(scan_back_kernel, width),
        grid=(nc + 1,),
        in_specs=[
            pl.BlockSpec((Q, cd), lambda i: (back(i), 0)),
            pl.BlockSpec((Q, cd), lambda i: (back(i), 0)),
            pl.BlockSpec((Q, LANES), lambda i: (back(i), 0)),
            pl.BlockSpec((Q, LANES), lambda i: (back(i), 0)),
            pl.BlockSpec((8, LANES), lambda i: (back(i), 0)),
            pl.BlockSpec((1, STATE, di), lambda i: (back(i), 0, 0)),
            whole(hin),
            whole(gin),
            pl.BlockSpec((Q, di), lambda i: (back(i), 0)),
            pl.BlockSpec((Q, cd), lambda i: (back(i) + 1, 0)),
            pl.BlockSpec((HALO, cd), lambda i: ((back(i) + 1) * (Q // HALO) - 1, 0)),
        ]
        + [whole(a) for a in args[11:]],
        out_specs=[
            pl.BlockSpec((Q, cdp), lambda i: (nc - i, 0)),
            pl.BlockSpec((8, cd), lambda i: (0, 0)),
            pl.BlockSpec((8, LANES), lambda i: (0, 0)),
        ],
        out_shape=[shape(t + Q, cdp, dtype=BF), shape(8, cd), shape(8, LANES)],
        scratch_shapes=[
            pltpu.VMEM((Q + 8, cd), F32),
            pltpu.VMEM((STATE, di), F32),
            pltpu.VMEM((LANES, Q), F32),
        ],
        compiler_params=VMEM,
        cost_estimate=cost(8 * t * d * di, xc, xc, xc, xc),
        name="scan_back",
    )(*args)

    g_x = dot_tn(nrm, dx).astype(BF)

    args = (dx, dnz, wa, wb, small, s, halo, cot)
    g_stream, msg = pl.pallas_call(
        stream_back_kernel,
        grid=(nc + 1,),
        in_specs=[
            pl.BlockSpec((Q, cdp), lambda i: (i, 0)),
            pl.BlockSpec((Q, d), lambda i: (at(i), 0)),
            whole(wa),
            whole(wb),
            whole(small),
            pl.BlockSpec((Q, d), lambda i: (at(i), 0)),
            whole(halo),
            pl.BlockSpec((Q, d), lambda i: (at(i), 0)),
        ],
        out_specs=[pl.BlockSpec((Q, d), lambda i: (at(i), 0)), pl.BlockSpec((HALO, d), lambda i: (0, 0))],
        out_shape=[shape(t, d), shape(HALO, d)],
        compiler_params=VMEM,
        cost_estimate=cost(2 * t * d * cdp, s, s, s, s, wa, wb),
        name="stream_back",
    )(*args)
    msg = lax.ppermute(msg, "hx", [(r + 1, r) for r in range(hx - 1)])
    g_stream = lax.dynamic_update_slice(g_stream, g_stream[t - HALO :] + msg, (t - HALO, 0))

    packed = jnp.concatenate([gconv, jnp.pad(ghead, ((0, 0), (0, LANES)))], axis=1)
    packed = all_sum(packed, n, hx)
    mine = lax.dynamic_slice_in_dim(packed[:, :cd], lax.axis_index("seq") * (cd // n), cd // n, 1)

    g_zo = over_hx(g_zo, hx)
    g_z, g_out = g_zo[:, :di], g_zo[:, di:].reshape(rows, per, d).transpose(1, 0, 2).reshape(rows * per, d)
    g_x = over_hx(scatter_rows(g_x, n, ca), hx)
    g_main = jnp.concatenate([g_z, g_x[:, :cd]], axis=1)
    g_dt = g_x[:, cd : cd + heads]
    g_norm = (
        jnp.sum(in_main.astype(F32) * g_main, axis=1) + jnp.sum(in_dt.astype(F32) * g_dt, axis=1)
    ) / norm_gain.astype(F32)
    g_gate = jnp.sum(out_weight.astype(F32) * g_out, axis=1) / gated_gain.astype(F32)
    return (
        out[None],
        g_stream[None],
        g_norm,
        g_main,
        g_dt,
        mine[:CONV],
        mine[CONV],
        packed[0, cd : cd + heads],
        packed[1, cd : cd + heads],
        packed[2, cd : cd + heads],
        g_gate,
        g_out,
    )


def solution(mesh):
    placed = (
        P("seq", "hx", None),
        P("seq", "hx", None),
        P("seq"),
        P("seq", None),
        P("seq", None),
        P(None, "seq"),
        P("seq"),
        P(),
        P(),
        P(),
        P("seq"),
        P("seq", None),
    )
    return jax.shard_map(
        shards,
        mesh=mesh,
        in_specs=placed,
        out_specs=(
            P("seq", "hx", None),
            P("seq", "hx", None),
            P("seq"),
            P("seq", None),
            P("seq", None),
            P(None, "seq"),
            P("seq"),
            P(),
            P(),
            P(),
            P("seq"),
            P("seq", None),
        ),
        check_vma=False,
    )
```

```python
import functools

import jax
import jax.numpy as jnp
from jax import lax
from jax.experimental import pallas as pl
from jax.experimental.pallas import tpu as pltpu
from jax.sharding import PartitionSpec as P

STATE = 128
CONV = 4
EPSILON = 1e-05
Q = 128
LANES = 128
GROUP = 256
WIDE = 2 * Q
HALO = 16
BF = jnp.bfloat16
F32 = jnp.float32
EXACT = lax.Precision.HIGHEST


def dot(a, b, precision=None):
    return lax.dot_general(
        a, b, (((1,), (0,)), ((), ())), precision=precision, preferred_element_type=F32
    )


def dot_nt(a, b):
    return lax.dot_general(a, b, (((1,), (1,)), ((), ())), preferred_element_type=F32)


def dot_tn(a, b):
    return lax.dot_general(a, b, (((0,), (0,)), ((), ())), preferred_element_type=F32)


def two_terms(v):
    hi = v.astype(BF)
    lo = (v - hi.astype(F32)).astype(BF)
    return jnp.concatenate([hi, lo], axis=1)


def softplus(v):
    return jnp.maximum(v, 0.0) + jnp.log1p(jnp.exp(-jnp.abs(v)))


def sigmoid(v):
    return 1.0 / (1.0 + jnp.exp(-v))


def three_terms(v):
    hi = v.astype(BF).astype(F32)
    mid = (v - hi).astype(BF).astype(F32)
    return hi, mid, (v - hi - mid).astype(BF).astype(F32)


def gap_left(cum, sign):
    hi, mid, lo = three_terms(sign * cum)
    lane = lax.broadcasted_iota(jnp.int32, cum.shape, 1)
    ones = jnp.where((lane >= 96) & (lane < 99), 1.0, 0.0)
    return (hi + pltpu.roll(mid, 32, 1) + pltpu.roll(lo, 64, 1) + ones).astype(BF)


def gap_right(cum_t, sign, heads, ref):
    hi, mid, lo = three_terms(sign * cum_t)
    zero = jnp.zeros((13, Q), F32)
    for h in range(heads):
        row = slice(h, h + 1)
        block = jnp.concatenate([hi[row], mid[row], lo[row], zero], axis=0)
        ref[96:112, Q * h : Q * (h + 1)] = block.astype(BF)


def root_of(v):
    return lax.rsqrt(jnp.mean(v * v, axis=-1, keepdims=True) + EPSILON)


def tri(rows, cols, keep):
    r = lax.broadcasted_iota(jnp.int32, (rows, cols), 0)
    c = lax.broadcasted_iota(jnp.int32, (rows, cols), 1)
    return keep(r, c)


def half_blocks(v, width):
    lane = lax.broadcasted_iota(jnp.int32, v.shape, 1)
    zero = jnp.zeros_like(v)
    return jnp.concatenate([jnp.where(lane < width, v, zero), jnp.where(lane >= width, v, zero)], axis=0)


def project_kernel(
    n,
    halo_ref,
    s_ref,
    wa_ref,
    wb_ref,
    hp_ref,
    ee_ref,
    shift_ref,
    nrm_ref,
    cin_ref,
    xc_ref,
    slope_ref,
    dtv_ref,
    cum_ref,
    base_ref,
    sloc_ref,
    fin_ref,
    tot_ref,
    small_ref,
    full,
    state,
    base,
):
    i = pl.program_id(0)
    cd = cin_ref.shape[1]
    di = fin_ref.shape[1]
    d, ca = wa_ref.shape
    rows = d // n

    def columns(lo, hi):
        if hi <= ca:
            return wa_ref[:, lo:hi]
        return wb_ref[:, lo - ca : hi - ca]

    @pl.when(i == 0)
    def _():
        small_ref[...] = jnp.zeros_like(small_ref)
        for k in range(n):
            piece = wb_ref[rows * k : rows * k + 8, cd + LANES - ca :].astype(F32)
            for row, size in ((0, d // n), (6, di // n)):
                small_ref[row : row + 1, size * k : size * (k + 1)] = piece[row : row + 1, :size]
            size = cd // n
            small_ref[1:6, size * k : size * (k + 1)] = piece[1:6, :size]
        h = halo_ref[...]
        nh = (h * root_of(h) * small_ref[0:1, :d]).astype(BF)
        nrm_ref[...] = jnp.zeros_like(nrm_ref)
        nrm_ref[WIDE - HALO :, :] = nh
        cin_ref[...] = jnp.zeros_like(cin_ref)
        ph = jnp.concatenate([dot(nh, columns(0, ca)), dot(nh, columns(ca, cd))], axis=1).astype(BF)
        cin_ref[WIDE - HALO :, :] = ph
        full[0:HALO, :] = ph
        state[...] = jnp.zeros_like(state)
        base[...] = jnp.zeros_like(base)

    @pl.when(i > 0)
    def _():
        s = s_ref[...]
        nrm = (s * root_of(s) * small_ref[0:1, :d]).astype(BF)
        nrm_ref[...] = nrm
        dtv = dot(nrm, columns(cd, cd + LANES)).astype(BF).astype(F32) + hp_ref[0:1, :]
        dtv_ref[...] = dtv
        step = softplus(dtv)
        lower = tri(Q, Q, lambda r, c: r >= c).astype(F32)
        weights, ends = [], []
        for p in range(WIDE // Q):
            part = slice(Q * p, Q * (p + 1))
            cum = dot(lower, hp_ref[1:2, :] * step[part], EXACT)
            cum_ref[part, :] = cum
            last = cum[Q - 1 : Q, :]
            base_ref[8 * p : 8 * (p + 1), :] = base[...]
            base[...] = base[...] + last
            weights.append(jnp.exp(last - cum) * step[part])
            ends.append(two_terms(jnp.broadcast_to(jnp.exp(last), (8, LANES))))
        weight = two_terms(jnp.concatenate(weights, axis=0))
        ends = jnp.concatenate(ends, axis=0)

        def conv(lo, hi):
            cin = dot(nrm, columns(lo, hi)).astype(BF)
            cin_ref[:, lo:hi] = cin
            full[HALO:, lo:hi] = cin
            earlier = [dot(shift_ref[...], full[Q * p : Q * (p + 1) + HALO, lo:hi]) for p in range(WIDE // Q)]
            summed = small_ref[5:6, lo:hi] + small_ref[4:5, lo:hi] * cin.astype(F32)
            for k in range(CONV - 1):
                rows_k = jnp.concatenate([e[Q * k : Q * (k + 1)] for e in earlier], axis=0)
                summed = summed + small_ref[k + 1 : k + 2, lo:hi] * rows_k
            full[0:HALO, lo:hi] = full[WIDE:, lo:hi]
            sig = sigmoid(summed)
            xc = summed * sig
            slope_ref[:, lo:hi] = (sig + xc * (1.0 - sig)).astype(BF)
            xcb = xc.astype(BF)
            xc_ref[:, lo:hi] = xcb
            return xc, xcb

        _, bc = conv(di, cd)
        bm = bc[:, :STATE]
        for lo in range(0, di, GROUP):
            cols = slice(lo, lo + GROUP)
            xc, _ = conv(lo, lo + GROUP)
            u = (dot(weight, ee_ref[:, cols]) * xc).astype(BF)
            fade = dot(ends, ee_ref[:, cols])
            now = state[:, cols]
            for p in range(WIDE // Q):
                part = slice(Q * p, Q * (p + 1))
                sloc_ref[p, :, cols] = now.astype(BF)
                now = now * fade[8 * p : 8 * p + 1] + dot_tn(bm[part], u[part])
            state[:, cols] = now

    @pl.when(i == pl.num_programs(0) - 1)
    def _():
        fin_ref[...] = state[...].astype(BF)
        tot_ref[...] = base[...]


def intra_kernel(width, xc_ref, dtv_ref, cum_ref, skip_ref, ee_ref, pick_ref, yi_ref, right):
    di = yi_ref.shape[1]

    @pl.when(pl.program_id(0) == 0)
    def _():
        right[...] = pick_ref[...]

    bm, cm = xc_ref[:, di : di + STATE], xc_ref[:, di + STATE :]
    cum = cum_ref[...]
    left = gap_left(cum, 1.0)
    gap_right(cum.T, -1.0, di // width, right)
    mix = jnp.where(tri(Q, Q, lambda r, c: r >= c), dot_nt(cm, bm), 0.0)
    step = two_terms(softplus(dtv_ref[...]))
    each = GROUP // width
    for lo in range(0, di, GROUP):
        cols = slice(lo, lo + GROUP)
        x = xc_ref[:, cols].astype(F32)
        ub = (dot(step, ee_ref[:, cols]) * x).astype(BF)
        first = lo // width
        gap = dot(left, right[:, Q * first : Q * (first + each)])
        parts = []
        for q in range(0, each, 2):
            two = [
                (jnp.exp(jnp.minimum(gap[:, Q * h : Q * (h + 1)], 0.0)) * mix).astype(BF) for h in (q, q + 1)
            ]
            pair = slice(q * width, (q + 2) * width)
            parts.append(dot(jnp.concatenate(two, axis=1), half_blocks(ub[:, pair], width)))
        yi_ref[:, cols] = (jnp.concatenate(parts, axis=1) + skip_ref[:, cols] * x).astype(BF)


def gate_kernel(
    n,
    yi_ref,
    nrm_ref,
    c_ref,
    cum_ref,
    base_ref,
    sloc_ref,
    hin_ref,
    s_ref,
    cot_ref,
    wzo_ref,
    small_ref,
    ee_ref,
    out_ref,
    mixed_ref,
    dsc_ref,
    dz_ref,
    start_ref,
    gst_ref,
    gst,
    wo,
    scan_s,
    z_s,
    weighted_s,
):
    i = pl.program_id(0)
    di = yi_ref.shape[1]
    d = s_ref.shape[1]

    @pl.when(i == 0)
    def _():
        gst[...] = jnp.zeros_like(gst)
        rows, per = d // n, di // d
        for k in range(n):
            for a in range(per):
                at = (per * k + a) * rows
                wo[at : at + rows, :] = wzo_ref[rows * k : rows * (k + 1), di + d * a : di + d * (a + 1)]

    halves = WIDE // Q
    nrm = nrm_ref[...]
    cm = c_ref[...]
    cotb = cot_ref[...].astype(BF)
    cum = cum_ref[...]
    bases = [base_ref[8 * p : 8 * p + 1, :] for p in range(halves)]
    ex_2 = two_terms(jnp.exp(cum))
    grow_2 = two_terms(jnp.concatenate([jnp.exp(cum[Q * p : Q * (p + 1)] + bases[p]) for p in range(halves)], axis=0))
    base_2 = two_terms(jnp.concatenate([jnp.broadcast_to(jnp.exp(b), (8, LANES)) for b in bases], axis=0))
    square = jnp.zeros((WIDE, LANES), F32)
    along = jnp.zeros((WIDE, LANES), F32)
    for lo in range(0, di, GROUP):
        cols = slice(lo, lo + GROUP)
        ee = ee_ref[:, cols]
        fade = dot(base_2, ee)
        inter = []
        for p in range(halves):
            start = (
                sloc_ref[p, :, cols].astype(F32) + fade[8 * p : 8 * p + 1] * hin_ref[:, cols].astype(F32)
            ).astype(BF)
            start_ref[p, :, cols] = start
            inter.append(dot(cm[Q * p : Q * (p + 1)], start))
        scb = (yi_ref[:, cols].astype(F32) + dot(ex_2, ee) * jnp.concatenate(inter, axis=0)).astype(BF)
        scan_s[:, cols] = scb
        z = dot(nrm, wzo_ref[:, cols])
        z_s[:, cols] = z
        gated = scb.astype(F32) * (z * sigmoid(z))
        weighted = small_ref[6:7, cols] * dot_nt(cotb, wo[cols, :])
        weighted_s[:, cols] = weighted
        for q in range(0, GROUP, LANES):
            g = gated[:, q : q + LANES]
            square = square + g * g
            along = along + g * weighted[:, q : q + LANES]
    inv = lax.rsqrt(jnp.sum(square, axis=-1, keepdims=True) / di + EPSILON)
    proj = inv * inv * (jnp.sum(along, axis=-1, keepdims=True) / di)
    for lo in range(0, di, GROUP):
        cols = slice(lo, lo + GROUP)
        scanned = scan_s[:, cols].astype(F32)
        z = z_s[:, cols]
        sig = sigmoid(z)
        silu = z * sig
        gated = scanned * silu
        mixed_ref[:, cols] = (gated * inv * small_ref[6:7, cols]).astype(BF)
        d_gated = inv * (weighted_s[:, cols] - gated * proj)
        dsc = (d_gated * silu).astype(BF)
        dsc_ref[:, cols] = dsc
        dz_ref[:, cols] = (d_gated * scanned * (sig + silu * (1.0 - sig))).astype(BF)
        grown = (dot(grow_2, ee_ref[:, cols]) * dsc.astype(F32)).astype(BF)
        gst[:, cols] = gst[:, cols] + dot_tn(cm, grown)
    out_ref[...] = s_ref[...] + dot(mixed_ref[...], wo[...])

    @pl.when(i == pl.num_programs(0) - 1)
    def _():
        gst_ref[...] = gst[...].astype(BF)


def scan_back_kernel(
    width,
    xc_ref,
    slope_ref,
    dtv_ref,
    cum_ref,
    start_ref,
    gin_ref,
    dsc_ref,
    cin_ref,
    prev_ref,
    small_ref,
    hp_ref,
    skip_ref,
    ee_ref,
    er_ref,
    hot_ref,
    pick_ref,
    shift_ref,
    d_ref,
    gconv_ref,
    ghead_ref,
    full_d,
    ds_state,
    kcol,
    right,
):
    i = pl.program_id(0)
    n = pl.num_programs(0) - 1
    di = dsc_ref.shape[1]
    cd = cin_ref.shape[1]

    def tap(k, cols=slice(None)):
        return small_ref[k + 1 : k + 2, cols]

    @pl.when(i == 0)
    def _():
        ds_state[...] = gin_ref[...].astype(F32)
        full_d[...] = jnp.zeros_like(full_d)
        kcol[...] = jnp.zeros_like(kcol)
        right[...] = pick_ref[...]
        gconv_ref[...] = jnp.zeros_like(gconv_ref)
        ghead_ref[...] = jnp.zeros_like(ghead_ref)

    @pl.when(i < n)
    def _():
        bm, cm = xc_ref[:, di : di + STATE], xc_ref[:, di + STATE :]
        dtv = dtv_ref[...]
        step = softplus(dtv)
        nega = hp_ref[1:2, :]
        cum = cum_ref[...]
        left = gap_left(cum, -1.0)
        gap_right(cum.T, 1.0, di // width, right)
        last = cum[Q - 1 : Q, :]
        causal = tri(Q, Q, lambda r, c: c >= r)
        mix_t = jnp.where(causal, dot_nt(bm, cm), 0.0)
        step_2 = two_terms(step)
        tail_2 = two_terms(jnp.exp(last - cum))
        ex_2 = two_terms(jnp.exp(cum))
        at_end = jnp.exp(last)
        end_2 = two_terms(jnp.broadcast_to(at_end, (8, LANES)))
        d_mix = jnp.zeros((Q, Q), F32)
        krow = jnp.zeros((Q, LANES), F32)
        d_b, d_c = jnp.zeros((Q, STATE), F32), jnp.zeros((Q, STATE), F32)
        sums = jnp.zeros((3 * Q, LANES), F32)
        row_sums = jnp.zeros((16, LANES), F32)

        def conv_back(cols, d_sum):
            full_d[0:Q, cols] = d_sum.astype(BF)
            laters = dot(shift_ref[...], full_d[:, cols])
            cin = cin_ref[:, cols].astype(F32)
            d_cin = tap(CONV - 1, cols) * d_sum
            gconv_ref[CONV - 1 : CONV, cols] += jnp.sum(d_sum * cin, axis=0, keepdims=True)
            gconv_ref[CONV : CONV + 1, cols] += jnp.sum(d_sum, axis=0, keepdims=True)
            for k in range(CONV - 1):
                later = laters[Q * k : Q * (k + 1)]
                d_cin = d_cin + tap(k, cols) * later
                gconv_ref[k : k + 1, cols] += jnp.sum(later * cin, axis=0, keepdims=True)
            d_ref[:, cols] = d_cin.astype(BF)
            full_d[Q:, cols] = full_d[0:HALO, cols]

        for lo in range(0, di, GROUP):
            cols = slice(lo, lo + GROUP)
            ee = ee_ref[:, cols]
            x = xc_ref[:, cols].astype(F32)
            dyb = dsc_ref[:, cols]
            dy = dyb.astype(F32)
            step_e = dot(step_2, ee)
            u = step_e * x
            ub = u.astype(BF)
            parts = []
            gap = dot(left, right[:, Q * (lo // width) : Q * ((lo + GROUP) // width)])
            for q in range(0, GROUP, 2 * width):
                pair = slice(q, q + 2 * width)
                dy_blocks = half_blocks(dyb[:, pair], width)
                d_m = dot_nt(ub[:, pair], dy_blocks)
                ms, ks = [], []
                first = (lo + q) // width
                for j in range(2):
                    h = first + j
                    at = Q * (h - lo // width)
                    fall = jnp.exp(jnp.minimum(gap[:, at : at + Q], 0.0))
                    m = mix_t * fall
                    d_one = d_m[:, Q * j : Q * (j + 1)]
                    d_mix = d_mix + d_one * fall
                    kb = (d_one * m).astype(BF)
                    kcol[h : h + 1, :] = jnp.sum(kb.astype(F32), axis=0, keepdims=True)
                    ms.append(m.astype(BF))
                    ks.append(kb)
                parts.append(dot(jnp.concatenate(ms, axis=1), dy_blocks))
                krow = krow + dot(jnp.concatenate(ks, axis=1), hot_ref[Q * first : Q * (first + 2), :])
            d_state = ds_state[:, cols]
            dsb = d_state.astype(BF)
            startb = start_ref[0, :, cols]
            tail_e = dot(tail_2, ee)
            from_state = tail_e * dot(bm, dsb)
            du = jnp.concatenate(parts, axis=1) + from_state
            edy = dot(ex_2, ee) * dy
            edyb = edy.astype(BF)
            d_b = d_b + dot_nt((tail_e * u).astype(BF), dsb)
            d_c = d_c + dot_nt(edyb, startb)
            three = jnp.concatenate([edy * dot(cm, startb), u * from_state, x * du], axis=0).astype(BF)
            sums = sums + dot(three, er_ref[cols, :])
            rows = jnp.concatenate(
                [
                    jnp.sum(startb.astype(F32) * d_state, axis=0, keepdims=True),
                    jnp.sum(dy * x, axis=0, keepdims=True),
                    jnp.zeros((6, GROUP), F32),
                ],
                axis=0,
            )
            rows_hi = rows.astype(BF)
            rows_lo = (rows - rows_hi.astype(F32)).astype(BF)
            row_sums = row_sums + dot(jnp.concatenate([rows_hi, rows_lo], axis=0), er_ref[cols, :])
            ds_state[:, cols] = dot(end_2, ee)[0:1] * d_state + dot_tn(cm, edyb)
            conv_back(cols, (step_e * du + skip_ref[:, cols] * dy) * slope_ref[:, cols].astype(F32))

        d_mixb = jnp.where(causal, d_mix, 0.0).astype(BF)
        d_bc = jnp.concatenate([d_b + dot(d_mixb, cm), d_c + dot_tn(d_mixb, bm)], axis=1)
        conv_back(slice(di, cd), d_bc * slope_ref[:, di:].astype(F32))
        upper = causal.astype(F32)
        strict = tri(Q, Q, lambda r, c: c < r).astype(F32)
        row_sums = row_sums[0:8] + row_sums[8:16]
        d_decay = (
            dot(upper, kcol[...].T + sums[:Q] - krow, EXACT)
            + dot(strict, sums[Q : 2 * Q], EXACT)
            + at_end * row_sums[0:1]
        )
        d_dt = (sums[2 * Q :] + nega * d_decay) * sigmoid(dtv)
        d_ref[:, cd:] = d_dt.astype(BF)
        ghead_ref[0:1, :] += jnp.sum(d_dt, axis=0, keepdims=True)
        ghead_ref[1:2, :] += jnp.sum(d_decay * nega * step, axis=0, keepdims=True)
        ghead_ref[2:3, :] += row_sums[1:2]

    @pl.when(i == n)
    def _():
        full_d[0:Q, :] = jnp.zeros((Q, cd), BF)
        cin = prev_ref[...].astype(F32)
        edge = jnp.zeros((HALO, cd), F32)
        for k in range(CONV - 1):
            later = dot(shift_ref[Q * (k + 1) - HALO : Q * (k + 1), :], full_d[...])
            edge = edge + tap(k) * later
            gconv_ref[k : k + 1, :] += jnp.sum(later * cin, axis=0, keepdims=True)
        d_ref[...] = jnp.zeros_like(d_ref)
        d_ref[Q - HALO :, :cd] = edge.astype(BF)


def stream_back_kernel(d_ref, dnz_ref, wa_ref, wb_ref, small_ref, s_ref, halo_ref, cot_ref, gs_ref, msg_ref):
    i = pl.program_id(0)
    d, ca = wa_ref.shape
    cdp = d_ref.shape[1]

    def through(dn, s):
        inv = root_of(s)
        weighted = small_ref[0:1, :d] * dn
        unit = s * inv
        return inv * (weighted - unit * jnp.mean(weighted * unit, axis=-1, keepdims=True))

    def back(rows):
        return dot_nt(rows[:, :ca], wa_ref[...]) + dot_nt(rows[:, ca:], wb_ref[:, : cdp - ca])

    @pl.when(i == 0)
    def _():
        msg_ref[...] = through(back(d_ref[Q - HALO :, :]), halo_ref[...])

    @pl.when(i > 0)
    def _():
        gs_ref[...] = cot_ref[...] + through(dnz_ref[...] + back(d_ref[...]), s_ref[...])


VMEM = pltpu.CompilerParams(vmem_limit_bytes=60 * 2**20)


def whole(a):
    return pl.BlockSpec(a.shape, lambda *_: (0,) * a.ndim)


def cost(flops, *arrays):
    return pl.CostEstimate(
        flops=int(flops), transcendentals=0, bytes_accessed=sum(a.size * a.dtype.itemsize for a in arrays)
    )


def shape(*dims, dtype=F32):
    return jax.ShapeDtypeStruct(dims, dtype)


def flip(v, axis, n, bit):
    return lax.ppermute(v, axis, [(s, s ^ bit) for s in range(n)])


def shift(v, axis, n, by):
    return lax.ppermute(v, axis, [(s, (s + by) % n) for s in range(n)])


def far_gather(v, n):
    far = n // 4
    z = lax.axis_index("seq") // 4
    got = [v] + [shift(v, "seq", n, 4 * k) for k in range(1, far)]
    buf = jnp.zeros((far,) + v.shape, v.dtype)
    for k in range(far):
        buf = lax.dynamic_update_slice_in_dim(buf, got[k][None], (z - k) % far, 0)
    return buf


def pair_gather(v, n, bit, axis):
    other = flip(v, "seq", n, bit)
    mine = (lax.axis_index("seq") // bit) % 2 == 0
    return jnp.where(mine, jnp.stack([v, other], axis), jnp.stack([other, v], axis))


def gather_rows(v, n, ca):
    a, b = v[:, :ca], v[:, ca:]
    b = pair_gather(b, n, 2, 0)
    a = far_gather(a, n)
    a = pair_gather(a, n, 2, 1)
    b = far_gather(b, n)
    a, b = pair_gather(a, n, 1, 2), pair_gather(b, n, 1, 2)
    return a.reshape(-1, a.shape[-1]), b.reshape(-1, b.shape[-1])


def pair_scatter(v, n, bit, axis):
    me = (lax.axis_index("seq") // bit) % 2
    mine = lax.dynamic_index_in_dim(v, me, axis, False)
    other = flip(lax.dynamic_index_in_dim(v, 1 - me, axis, False), "seq", n, bit)
    return (mine.astype(F32) + other.astype(F32)).astype(BF)


def far_scatter(v, n):
    far = n // 4
    z = lax.axis_index("seq") // 4
    total = lax.dynamic_index_in_dim(v, z, 0, False).astype(F32)
    for k in range(1, far):
        sent = lax.dynamic_index_in_dim(v, (z + k) % far, 0, False)
        total = total + shift(sent, "seq", n, 4 * k).astype(F32)
    return total.astype(BF)


def over_hx(v, hx):
    if hx == 2:
        b = v.astype(BF)
        return b.astype(F32) + flip(b, "hx", hx, 1).astype(F32)
    return lax.psum(v.astype(F32), "hx")


def sum_steps(n, hx):
    steps = []
    for axis, size in (("seq", n), ("hx", hx)):
        bit = 1
        while bit < size:
            steps.append(functools.partial(lambda axis, size, bit, v: v + flip(v, axis, size, bit), axis, size, bit))
            bit *= 2
    return steps


def together(*values):
    return lax.optimization_barrier(values)


def shards(
    stream,
    cotangent,
    norm_gain,
    in_main,
    in_dt,
    conv_weight,
    conv_bias,
    dt_bias,
    a_log,
    skip_gain,
    gated_gain,
    out_weight,
):
    n, hx = lax.axis_size("seq"), lax.axis_size("hx")
    s, cot = stream[0], cotangent[0]
    t, d = s.shape
    heads = in_dt.shape[1]
    di = out_weight.shape[0] * n
    cd = conv_weight.shape[1] * n
    width = di // heads
    nc = t // Q
    cdp = cd + LANES
    rows = in_main.shape[0]
    per = di // d

    def lanes(v):
        return jnp.pad(v, ((0, 0), (0, LANES - v.shape[1])))

    small = jnp.concatenate(
        [lanes(norm_gain[None]), lanes(conv_weight), lanes(conv_bias[None]), lanes(gated_gain[None])], axis=0
    )
    small = jnp.pad(small, ((0, rows - small.shape[0]), (0, 0)))
    wx = jnp.concatenate([in_main[:, di:], lanes(in_dt), small], axis=1)
    ca = wx.shape[1] * 2 // 3 // GROUP * GROUP
    wa, wb = gather_rows(wx, n, ca)
    wzo = jnp.concatenate([in_main[:, :di], out_weight.reshape(per, rows, d).transpose(1, 0, 2).reshape(rows, di)], axis=1)
    wzo = lax.all_gather(wzo, "seq", axis=0, tiled=True)
    halo = lax.ppermute(s[t - HALO :], "hx", [(r, r + 1) for r in range(hx - 1)])

    head_rows = jnp.pad(jnp.stack([dt_bias, -jnp.exp(a_log)]), ((0, 6), (0, LANES - heads)))
    owner = jnp.arange(di, dtype=jnp.int32) // width
    er = (owner[:, None] == jnp.arange(LANES, dtype=jnp.int32)[None, :]).astype(BF)
    one = (jnp.arange(LANES, dtype=jnp.int32)[:, None] == owner[None, :]).astype(BF)
    ee = jnp.concatenate([one, one], axis=0)
    skip = jnp.repeat(skip_gain, width)[None, :]
    hot = (
        (jnp.arange(heads * Q, dtype=jnp.int32) // Q)[:, None] == jnp.arange(LANES, dtype=jnp.int32)[None, :]
    ).astype(BF)

    block = jnp.arange(heads * Q, dtype=jnp.int32) // Q
    which = jnp.arange(LANES, dtype=jnp.int32)
    pick = ((which[:, None] % 32 == block[None, :]) & (which[:, None] < 96)).astype(BF)
    row = jnp.arange((CONV - 1) * Q, dtype=jnp.int32)[:, None]
    col = jnp.arange(Q + HALO, dtype=jnp.int32)[None, :]
    ahead = (col == HALO + row % Q - (CONV - 1) + row // Q).astype(BF)
    behind = (col == row % Q + (CONV - 1) - row // Q).astype(BF)
    nw = t // WIDE
    two = WIDE // Q

    def at(i):
        return jnp.maximum(i - 1, 0)

    wa, er, ee, skip, hot, pick, ahead, behind = together(wa, er, ee, skip, hot, pick, ahead, behind)
    args = (halo, s, wa, wb, head_rows, ee, ahead)
    nrm, cin, xc, slope, dtv, cum, base, sloc, fin, tot, small = pl.pallas_call(
        functools.partial(project_kernel, n),
        grid=(nw + 1,),
        in_specs=[whole(halo), pl.BlockSpec((WIDE, d), lambda i: (at(i), 0))] + [whole(a) for a in args[2:]],
        out_specs=[
            pl.BlockSpec((WIDE, d), lambda i: (i, 0)),
            pl.BlockSpec((WIDE, cd), lambda i: (i, 0)),
            pl.BlockSpec((WIDE, cd), lambda i: (at(i), 0)),
            pl.BlockSpec((WIDE, cd), lambda i: (at(i), 0)),
            pl.BlockSpec((WIDE, LANES), lambda i: (at(i), 0)),
            pl.BlockSpec((WIDE, LANES), lambda i: (at(i), 0)),
            pl.BlockSpec((8 * two, LANES), lambda i: (at(i), 0)),
            pl.BlockSpec((two, STATE, di), lambda i: (at(i), 0, 0)),
            pl.BlockSpec((STATE, di), lambda i: (0, 0)),
            pl.BlockSpec((8, LANES), lambda i: (0, 0)),
            pl.BlockSpec((8, cd), lambda i: (0, 0)),
        ],
        out_shape=[
            shape(t + WIDE, d, dtype=BF),
            shape(t + WIDE, cd, dtype=BF),
            shape(t, cd, dtype=BF),
            shape(t, cd, dtype=BF),
            shape(t, LANES),
            shape(t, LANES),
            shape(8 * nc, LANES),
            shape(nc, STATE, di, dtype=BF),
            shape(STATE, di, dtype=BF),
            shape(8, LANES),
            shape(8, cd),
        ],
        scratch_shapes=[pltpu.VMEM((WIDE + HALO, cd), BF), pltpu.VMEM((STATE, di), F32), pltpu.VMEM((8, LANES), F32)],
        compiler_params=VMEM,
        cost_estimate=cost(3 * t * d * cdp, s, wa, wb, s, s),
        name="project",
    )(*args)

    def carry(v, step_by):
        links = [(r, r + step_by) for r in range(hx) if 0 <= r + step_by < hx]
        got = lax.ppermute(v, "hx", links)
        total = got
        if hx > 2:
            fade = jnp.repeat(jnp.exp(tot[0, :heads]), width)[None, :]
            total = got.astype(F32)
            for _ in range(hx - 2):
                got = lax.ppermute((fade * got.astype(F32)).astype(BF), "hx", links)
                total = total + got.astype(F32)
            total = total.astype(BF)
        return total

    hin = carry(fin, 1)

    args = (xc, dtv, cum, skip, ee, pick)
    yi = pl.pallas_call(
        functools.partial(intra_kernel, width),
        grid=(nc,),
        in_specs=[
            pl.BlockSpec((Q, cd), lambda i: (i, 0)),
            pl.BlockSpec((Q, LANES), lambda i: (i, 0)),
            pl.BlockSpec((Q, LANES), lambda i: (i, 0)),
            whole(skip),
            whole(ee),
            whole(pick),
        ],
        out_specs=pl.BlockSpec((Q, di), lambda i: (i, 0)),
        out_shape=shape(t, di, dtype=BF),
        scratch_shapes=[pltpu.VMEM(pick.shape, BF)],
        compiler_params=VMEM,
        cost_estimate=cost(2 * t * d * di, xc, xc),
        name="intra",
    )(*args)

    args = (yi, nrm, xc, cum, base, sloc, hin, s, cot, wzo, small, ee)
    out, mixed, dsc, dz, start, gst = pl.pallas_call(
        functools.partial(gate_kernel, n),
        grid=(nw,),
        in_specs=[
            pl.BlockSpec((WIDE, di), lambda i: (i, 0)),
            pl.BlockSpec((WIDE, d), lambda i: (i + 1, 0)),
            pl.BlockSpec((WIDE, STATE), lambda i: (i, cd // STATE - 1)),
            pl.BlockSpec((WIDE, LANES), lambda i: (i, 0)),
            pl.BlockSpec((8 * two, LANES), lambda i: (i, 0)),
            pl.BlockSpec((two, STATE, di), lambda i: (i, 0, 0)),
            whole(hin),
            pl.BlockSpec((WIDE, d), lambda i: (i, 0)),
            pl.BlockSpec((WIDE, d), lambda i: (i, 0)),
            whole(wzo),
            whole(small),
            whole(ee),
        ],
        out_specs=[
            pl.BlockSpec((WIDE, d), lambda i: (i, 0)),
            pl.BlockSpec((WIDE, di), lambda i: (i, 0)),
            pl.BlockSpec((WIDE, di), lambda i: (i, 0)),
            pl.BlockSpec((WIDE, di), lambda i: (i, 0)),
            pl.BlockSpec((two, STATE, di), lambda i: (i, 0, 0)),
            pl.BlockSpec((STATE, di), lambda i: (0, 0)),
        ],
        out_shape=[
            shape(t, d),
            shape(t, di, dtype=BF),
            shape(t, di, dtype=BF),
            shape(t, di, dtype=BF),
            shape(nc, STATE, di, dtype=BF),
            shape(STATE, di, dtype=BF),
        ],
        scratch_shapes=[
            pltpu.VMEM((STATE, di), F32),
            pltpu.VMEM((di, d), BF),
            pltpu.VMEM((WIDE, di), BF),
            pltpu.VMEM((WIDE, di), F32),
            pltpu.VMEM((WIDE, di), F32),
        ],
        compiler_params=VMEM,
        cost_estimate=cost(6 * t * d * di, yi, yi, yi, xc, s, s, s),
        name="gate",
    )(*args)

    gin = carry(gst, -1)
    g_z = dot_tn(nrm[WIDE:], dz).astype(BF)
    g_out = dot_tn(mixed, cot.astype(BF)).astype(BF)
    g_zo = jnp.concatenate([g_z, g_out.reshape(n, per, rows, d).transpose(0, 2, 1, 3).reshape(d, di)], axis=1)
    g_zo = lax.psum_scatter(g_zo, "seq", scatter_dimension=0, tiled=True)
    args = (xc, slope, dtv, cum, start, gin, dsc, cin, cin, small, head_rows, skip, ee, er, hot, pick, behind)

    def back(i):
        return jnp.maximum(nc - 1 - i, 0)

    dx, gconv, ghead = pl.pallas_call(
        functools.partial(scan_back_kernel, width),
        grid=(nc + 1,),
        in_specs=[
            pl.BlockSpec((Q, cd), lambda i: (back(i), 0)),
            pl.BlockSpec((Q, cd), lambda i: (back(i), 0)),
            pl.BlockSpec((Q, LANES), lambda i: (back(i), 0)),
            pl.BlockSpec((Q, LANES), lambda i: (back(i), 0)),
            pl.BlockSpec((1, STATE, di), lambda i: (back(i), 0, 0)),
            whole(gin),
            pl.BlockSpec((Q, di), lambda i: (back(i), 0)),
            pl.BlockSpec((Q, cd), lambda i: (back(i) + two, 0)),
            pl.BlockSpec((HALO, cd), lambda i: (WIDE // HALO - 1, 0)),
        ]
        + [whole(a) for a in args[9:]],
        out_specs=[
            pl.BlockSpec((Q, cdp), lambda i: (nc - i, 0)),
            pl.BlockSpec((8, cd), lambda i: (0, 0)),
            pl.BlockSpec((8, LANES), lambda i: (0, 0)),
        ],
        out_shape=[shape(t + Q, cdp, dtype=BF), shape(8, cd), shape(8, LANES)],
        scratch_shapes=[
            pltpu.VMEM((Q + HALO, cd), BF),
            pltpu.VMEM((STATE, di), F32),
            pltpu.VMEM((LANES, Q), F32),
            pltpu.VMEM(pick.shape, BF),
        ],
        compiler_params=VMEM,
        cost_estimate=cost(8 * t * d * di, xc, xc, xc, xc),
        name="scan_back",
    )(*args)

    packed = jnp.concatenate([gconv, jnp.pad(ghead, ((0, 0), (0, LANES)))], axis=1)
    steps = sum_steps(n, hx)
    g_x = dot_tn(nrm[WIDE - Q :], dx).astype(BF)
    g_x, dz, packed = together(g_x, dz, packed)
    g_x = pair_scatter(g_x.reshape(n // 4, 2, 2, rows, cdp), n, 1, 2)
    packed = steps[0](packed)
    dnz = dot_nt(dz, wzo[:, :di])
    g_x, packed, dnz, dx = together(g_x, packed, dnz, dx)
    g_x = pair_scatter(g_x, n, 2, 1)
    packed = steps[1](packed)

    args = (dx, dnz, wa, wb, small, s, halo, cot)
    g_stream, msg = pl.pallas_call(
        stream_back_kernel,
        grid=(nc + 1,),
        in_specs=[
            pl.BlockSpec((Q, cdp), lambda i: (i, 0)),
            pl.BlockSpec((Q, d), lambda i: (at(i), 0)),
            whole(wa),
            whole(wb),
            whole(small),
            pl.BlockSpec((Q, d), lambda i: (at(i), 0)),
            whole(halo),
            pl.BlockSpec((Q, d), lambda i: (at(i), 0)),
        ],
        out_specs=[pl.BlockSpec((Q, d), lambda i: (at(i), 0)), pl.BlockSpec((HALO, d), lambda i: (0, 0))],
        out_shape=[shape(t, d), shape(HALO, d)],
        compiler_params=VMEM,
        cost_estimate=cost(2 * t * d * cdp, s, s, s, s, wa, wb),
        name="stream_back",
    )(*args)
    g_x, packed, msg, g_zo = together(g_x, packed, msg, g_zo)
    g_zo = over_hx(g_zo, hx)
    g_x = far_scatter(g_x, n)
    for step in steps[2:-1]:
        packed = step(packed)
    msg = lax.ppermute(msg, "hx", [(r + 1, r) for r in range(hx - 1)])
    g_x, packed, msg, g_zo = together(g_x, packed, msg, g_zo)
    g_x = over_hx(g_x, hx)
    packed = steps[-1](packed)
    g_stream = lax.dynamic_update_slice(g_stream, g_stream[t - HALO :] + msg, (t - HALO, 0))
    mine = lax.dynamic_slice_in_dim(packed[:, :cd], lax.axis_index("seq") * (cd // n), cd // n, 1)
    g_z, g_out = g_zo[:, :di], g_zo[:, di:].reshape(rows, per, d).transpose(1, 0, 2).reshape(rows * per, d)
    g_main = jnp.concatenate([g_z, g_x[:, :cd]], axis=1)
    g_dt = g_x[:, cd : cd + heads]
    g_norm = (
        jnp.sum(in_main.astype(F32) * g_main, axis=1) + jnp.sum(in_dt.astype(F32) * g_dt, axis=1)
    ) / norm_gain.astype(F32)
    g_gate = jnp.sum(out_weight.astype(F32) * g_out, axis=1) / gated_gain.astype(F32)
    return (
        out[None],
        g_stream[None],
        g_norm,
        g_main,
        g_dt,
        mine[:CONV],
        mine[CONV],
        packed[0, cd : cd + heads],
        packed[1, cd : cd + heads],
        packed[2, cd : cd + heads],
        g_gate,
        g_out,
    )


def solution(mesh):
    placed = (
        P("seq", "hx", None),
        P("seq", "hx", None),
        P("seq"),
        P("seq", None),
        P("seq", None),
        P(None, "seq"),
        P("seq"),
        P(),
        P(),
        P(),
        P("seq"),
        P("seq", None),
    )
    return jax.shard_map(
        shards,
        mesh=mesh,
        in_specs=placed,
        out_specs=(
            P("seq", "hx", None),
            P("seq", "hx", None),
            P("seq"),
            P("seq", None),
            P("seq", None),
            P(None, "seq"),
            P("seq"),
            P(),
            P(),
            P(),
            P("seq"),
            P("seq", None),
        ),
        check_vma=False,
    )
```

```python
import functools

import jax
import jax.numpy as jnp
from jax import lax
from jax.experimental import pallas as pl
from jax.experimental.pallas import tpu as pltpu
from jax.sharding import PartitionSpec as P

STATE = 128
CONV = 4
EPSILON = 1e-05
Q = 128
LANES = 128
GROUP = 256
WIDE = 2 * Q
HALO = 16
BF = jnp.bfloat16
F32 = jnp.float32


def dot(a, b):
    return lax.dot_general(a, b, (((1,), (0,)), ((), ())), preferred_element_type=F32)


def dot_nt(a, b):
    return lax.dot_general(a, b, (((1,), (1,)), ((), ())), preferred_element_type=F32)


def dot_tn(a, b):
    return lax.dot_general(a, b, (((0,), (0,)), ((), ())), preferred_element_type=F32)


def two_terms(v):
    hi = v.astype(BF)
    lo = (v - hi.astype(F32)).astype(BF)
    return jnp.concatenate([hi, lo], axis=1)


def softplus(v):
    return jnp.maximum(v, 0.0) + jnp.log1p(jnp.exp(-jnp.abs(v)))


def sigmoid(v):
    return 1.0 / (1.0 + jnp.exp(-v))


def three_terms(v):
    hi = v.astype(BF).astype(F32)
    mid = (v - hi).astype(BF).astype(F32)
    return hi, mid, (v - hi - mid).astype(BF).astype(F32)


def choose_sum(chosen, v):
    w = v.shape[1]
    got = dot(chosen.astype(BF), jnp.concatenate(three_terms(v), axis=1).astype(BF))
    return got[:, :w] + got[:, w : 2 * w] + got[:, 2 * w :]


def gap_left(cum, sign):
    hi, mid, lo = three_terms(sign * cum)
    lane = lax.broadcasted_iota(jnp.int32, cum.shape, 1)
    ones = jnp.where((lane >= 96) & (lane < 99), 1.0, 0.0)
    return (hi + pltpu.roll(mid, 32, 1) + pltpu.roll(lo, 64, 1) + ones).astype(BF)


def gap_right(cum_t, sign, heads, ref):
    hi, mid, lo = three_terms(sign * cum_t)
    zero = jnp.zeros((13, Q), F32)
    for h in range(heads):
        row = slice(h, h + 1)
        block = jnp.concatenate([hi[row], mid[row], lo[row], zero], axis=0)
        ref[96:112, Q * h : Q * (h + 1)] = block.astype(BF)


def root_of(v):
    return lax.rsqrt(jnp.mean(v * v, axis=-1, keepdims=True) + EPSILON)


def tri(rows, cols, keep):
    r = lax.broadcasted_iota(jnp.int32, (rows, cols), 0)
    c = lax.broadcasted_iota(jnp.int32, (rows, cols), 1)
    return keep(r, c)


def half_blocks(v, width):
    lane = lax.broadcasted_iota(jnp.int32, v.shape, 1)
    zero = jnp.zeros_like(v)
    return jnp.concatenate([jnp.where(lane < width, v, zero), jnp.where(lane >= width, v, zero)], axis=0)


def project_kernel(
    n,
    halo_ref,
    s_ref,
    wa_ref,
    wb_ref,
    hp_ref,
    ee_ref,
    shift_ref,
    nrm_ref,
    cin_ref,
    xc_ref,
    slope_ref,
    dtv_ref,
    cum_ref,
    base_ref,
    sloc_ref,
    fin_ref,
    tot_ref,
    small_ref,
    full,
    state,
    base,
):
    i = pl.program_id(0)
    cd = cin_ref.shape[1]
    di = fin_ref.shape[1]
    d, ca = wa_ref.shape
    rows = d // n

    def columns(lo, hi):
        if hi <= ca:
            return wa_ref[:, lo:hi]
        return wb_ref[:, lo - ca : hi - ca]

    @pl.when(i == 0)
    def _():
        small_ref[...] = jnp.zeros_like(small_ref)
        for k in range(n):
            piece = wb_ref[rows * k : rows * k + 8, cd + LANES - ca :].astype(F32)
            for row, size in ((0, d // n), (6, di // n)):
                small_ref[row : row + 1, size * k : size * (k + 1)] = piece[row : row + 1, :size]
            size = cd // n
            small_ref[1:6, size * k : size * (k + 1)] = piece[1:6, :size]
        h = halo_ref[...]
        nh = (h * root_of(h) * small_ref[0:1, :d]).astype(BF)
        nrm_ref[...] = jnp.zeros_like(nrm_ref)
        nrm_ref[WIDE - HALO :, :] = nh
        cin_ref[...] = jnp.zeros_like(cin_ref)
        ph = jnp.concatenate([dot(nh, columns(0, ca)), dot(nh, columns(ca, cd))], axis=1).astype(BF)
        cin_ref[WIDE - HALO :, :] = ph
        full[0:HALO, :] = ph
        state[...] = jnp.zeros_like(state)
        base[...] = jnp.zeros_like(base)

    @pl.when(i > 0)
    def _():
        s = s_ref[...]
        nrm = (s * root_of(s) * small_ref[0:1, :d]).astype(BF)
        nrm_ref[...] = nrm
        dtv = dot(nrm, columns(cd, cd + LANES)).astype(BF).astype(F32) + hp_ref[0:1, :]
        dtv_ref[...] = dtv
        step = softplus(dtv)
        lower = tri(Q, Q, lambda r, c: r >= c).astype(F32)
        weights, ends = [], []
        for p in range(WIDE // Q):
            part = slice(Q * p, Q * (p + 1))
            cum = choose_sum(lower, hp_ref[1:2, :] * step[part])
            cum_ref[part, :] = cum
            last = cum[Q - 1 : Q, :]
            base_ref[8 * p : 8 * (p + 1), :] = base[...]
            base[...] = base[...] + last
            weights.append(jnp.exp(last - cum) * step[part])
            ends.append(two_terms(jnp.broadcast_to(jnp.exp(last), (8, LANES))))
        weight = two_terms(jnp.concatenate(weights, axis=0))
        ends = jnp.concatenate(ends, axis=0)

        def conv(lo, hi):
            cin = dot(nrm, columns(lo, hi)).astype(BF)
            cin_ref[:, lo:hi] = cin
            full[HALO:, lo:hi] = cin
            earlier = [dot(shift_ref[...], full[Q * p : Q * (p + 1) + HALO, lo:hi]) for p in range(WIDE // Q)]
            summed = small_ref[5:6, lo:hi] + small_ref[4:5, lo:hi] * cin.astype(F32)
            for k in range(CONV - 1):
                rows_k = jnp.concatenate([e[Q * k : Q * (k + 1)] for e in earlier], axis=0)
                summed = summed + small_ref[k + 1 : k + 2, lo:hi] * rows_k
            full[0:HALO, lo:hi] = full[WIDE:, lo:hi]
            sig = sigmoid(summed)
            xc = summed * sig
            slope_ref[:, lo:hi] = (sig + xc * (1.0 - sig)).astype(BF)
            xcb = xc.astype(BF)
            xc_ref[:, lo:hi] = xcb
            return xc, xcb

        _, bc = conv(di, cd)
        bm = bc[:, :STATE]
        for lo in range(0, di, GROUP):
            cols = slice(lo, lo + GROUP)
            xc, _ = conv(lo, lo + GROUP)
            u = (dot(weight, ee_ref[:, cols]) * xc).astype(BF)
            fade = dot(ends, ee_ref[:, cols])
            now = state[:, cols]
            for p in range(WIDE // Q):
                part = slice(Q * p, Q * (p + 1))
                sloc_ref[p, :, cols] = now.astype(BF)
                now = now * fade[8 * p : 8 * p + 1] + dot_tn(bm[part], u[part])
            state[:, cols] = now

    @pl.when(i == pl.num_programs(0) - 1)
    def _():
        fin_ref[...] = state[...].astype(BF)
        tot_ref[...] = base[...]


def intra_kernel(width, xc_ref, dtv_ref, cum_ref, skip_ref, ee_ref, pick_ref, yi_ref, right):
    di = yi_ref.shape[1]

    @pl.when(pl.program_id(0) == 0)
    def _():
        right[...] = pick_ref[...]

    bm, cm = xc_ref[:, di : di + STATE], xc_ref[:, di + STATE :]
    cum = cum_ref[...]
    left = gap_left(cum, 1.0)
    gap_right(cum.T, -1.0, di // width, right)
    mix = jnp.where(tri(Q, Q, lambda r, c: r >= c), dot_nt(cm, bm), 0.0)
    step = two_terms(softplus(dtv_ref[...]))
    each = GROUP // width
    for lo in range(0, di, GROUP):
        cols = slice(lo, lo + GROUP)
        x = xc_ref[:, cols].astype(F32)
        ub = (dot(step, ee_ref[:, cols]) * x).astype(BF)
        first = lo // width
        gap = dot(left, right[:, Q * first : Q * (first + each)])
        parts = []
        for q in range(0, each, 2):
            two = [
                (jnp.exp(jnp.minimum(gap[:, Q * h : Q * (h + 1)], 0.0)) * mix).astype(BF) for h in (q, q + 1)
            ]
            pair = slice(q * width, (q + 2) * width)
            parts.append(dot(jnp.concatenate(two, axis=1), half_blocks(ub[:, pair], width)))
        yi_ref[:, cols] = (jnp.concatenate(parts, axis=1) + skip_ref[:, cols] * x).astype(BF)


def gate_kernel(
    n,
    yi_ref,
    nrm_ref,
    c_ref,
    cum_ref,
    base_ref,
    sloc_ref,
    hin_ref,
    s_ref,
    cot_ref,
    wzo_ref,
    small_ref,
    ee_ref,
    out_ref,
    mixed_ref,
    dsc_ref,
    dz_ref,
    start_ref,
    gst_ref,
    gst,
    wo,
    scan_s,
    z_s,
    weighted_s,
):
    i = pl.program_id(0)
    di = yi_ref.shape[1]
    d = s_ref.shape[1]

    @pl.when(i == 0)
    def _():
        gst[...] = jnp.zeros_like(gst)
        rows, per = d // n, di // d
        for k in range(n):
            for a in range(per):
                at = (per * k + a) * rows
                wo[at : at + rows, :] = wzo_ref[rows * k : rows * (k + 1), di + d * a : di + d * (a + 1)]

    halves = WIDE // Q
    nrm = nrm_ref[...]
    cm = c_ref[...]
    cotb = cot_ref[...].astype(BF)
    cum = cum_ref[...]
    bases = [base_ref[8 * p : 8 * p + 1, :] for p in range(halves)]
    ex_2 = two_terms(jnp.exp(cum))
    grow_2 = two_terms(jnp.concatenate([jnp.exp(cum[Q * p : Q * (p + 1)] + bases[p]) for p in range(halves)], axis=0))
    base_2 = two_terms(jnp.concatenate([jnp.broadcast_to(jnp.exp(b), (8, LANES)) for b in bases], axis=0))
    square = jnp.zeros((WIDE, LANES), F32)
    along = jnp.zeros((WIDE, LANES), F32)
    for lo in range(0, di, GROUP):
        cols = slice(lo, lo + GROUP)
        ee = ee_ref[:, cols]
        fade = dot(base_2, ee)
        inter = []
        for p in range(halves):
            start = (
                sloc_ref[p, :, cols].astype(F32) + fade[8 * p : 8 * p + 1] * hin_ref[:, cols].astype(F32)
            ).astype(BF)
            start_ref[p, :, cols] = start
            inter.append(dot(cm[Q * p : Q * (p + 1)], start))
        scb = (yi_ref[:, cols].astype(F32) + dot(ex_2, ee) * jnp.concatenate(inter, axis=0)).astype(BF)
        scan_s[:, cols] = scb
        z = dot(nrm, wzo_ref[:, cols])
        z_s[:, cols] = z
        gated = scb.astype(F32) * (z * sigmoid(z))
        weighted = small_ref[6:7, cols] * dot_nt(cotb, wo[cols, :])
        weighted_s[:, cols] = weighted
        for q in range(0, GROUP, LANES):
            g = gated[:, q : q + LANES]
            square = square + g * g
            along = along + g * weighted[:, q : q + LANES]
    inv = lax.rsqrt(jnp.sum(square, axis=-1, keepdims=True) / di + EPSILON)
    proj = inv * inv * (jnp.sum(along, axis=-1, keepdims=True) / di)
    for lo in range(0, di, GROUP):
        cols = slice(lo, lo + GROUP)
        scanned = scan_s[:, cols].astype(F32)
        z = z_s[:, cols]
        sig = sigmoid(z)
        silu = z * sig
        gated = scanned * silu
        mixed_ref[:, cols] = (gated * inv * small_ref[6:7, cols]).astype(BF)
        d_gated = inv * (weighted_s[:, cols] - gated * proj)
        dsc = (d_gated * silu).astype(BF)
        dsc_ref[:, cols] = dsc
        dz_ref[:, cols] = (d_gated * scanned * (sig + silu * (1.0 - sig))).astype(BF)
        grown = (dot(grow_2, ee_ref[:, cols]) * dsc.astype(F32)).astype(BF)
        gst[:, cols] = gst[:, cols] + dot_tn(cm, grown)
    out_ref[...] = s_ref[...] + dot(mixed_ref[...], wo[...])

    @pl.when(i == pl.num_programs(0) - 1)
    def _():
        gst_ref[...] = gst[...].astype(BF)


def scan_back_kernel(
    width,
    xc_ref,
    slope_ref,
    dtv_ref,
    cum_ref,
    start_ref,
    gin_ref,
    dsc_ref,
    cin_ref,
    prev_ref,
    small_ref,
    hp_ref,
    skip_ref,
    ee_ref,
    er_ref,
    hot_ref,
    pick_ref,
    shift_ref,
    d_ref,
    gconv_ref,
    ghead_ref,
    full_d,
    ds_state,
    kcol,
    right,
):
    i = pl.program_id(0)
    n = pl.num_programs(0) - 1
    di = dsc_ref.shape[1]
    cd = cin_ref.shape[1]

    def tap(k, cols=slice(None)):
        return small_ref[k + 1 : k + 2, cols]

    @pl.when(i == 0)
    def _():
        ds_state[...] = gin_ref[...].astype(F32)
        full_d[...] = jnp.zeros_like(full_d)
        kcol[...] = jnp.zeros_like(kcol)
        right[...] = pick_ref[...]
        gconv_ref[...] = jnp.zeros_like(gconv_ref)
        ghead_ref[...] = jnp.zeros_like(ghead_ref)

    @pl.when(i < n)
    def _():
        bm, cm = xc_ref[:, di : di + STATE], xc_ref[:, di + STATE :]
        dtv = dtv_ref[...]
        step = softplus(dtv)
        nega = hp_ref[1:2, :]
        cum = cum_ref[...]
        left = gap_left(cum, -1.0)
        gap_right(cum.T, 1.0, di // width, right)
        last = cum[Q - 1 : Q, :]
        causal = tri(Q, Q, lambda r, c: c >= r)
        mix_t = jnp.where(causal, dot_nt(bm, cm), 0.0)
        step_2 = two_terms(step)
        tail_2 = two_terms(jnp.exp(last - cum))
        ex_2 = two_terms(jnp.exp(cum))
        at_end = jnp.exp(last)
        end_2 = two_terms(jnp.broadcast_to(at_end, (8, LANES)))
        d_mix = jnp.zeros((Q, Q), F32)
        krow = jnp.zeros((Q, LANES), F32)
        d_b, d_c = jnp.zeros((Q, STATE), F32), jnp.zeros((Q, STATE), F32)
        sums = jnp.zeros((3 * Q, LANES), F32)
        row_sums = jnp.zeros((16, LANES), F32)

        def conv_back(cols, d_sum):
            full_d[0:Q, cols] = d_sum.astype(BF)
            laters = dot(shift_ref[...], full_d[:, cols])
            cin = cin_ref[:, cols].astype(F32)
            d_cin = tap(CONV - 1, cols) * d_sum
            gconv_ref[CONV - 1 : CONV, cols] += jnp.sum(d_sum * cin, axis=0, keepdims=True)
            gconv_ref[CONV : CONV + 1, cols] += jnp.sum(d_sum, axis=0, keepdims=True)
            for k in range(CONV - 1):
                later = laters[Q * k : Q * (k + 1)]
                d_cin = d_cin + tap(k, cols) * later
                gconv_ref[k : k + 1, cols] += jnp.sum(later * cin, axis=0, keepdims=True)
            d_ref[:, cols] = d_cin.astype(BF)
            full_d[Q:, cols] = full_d[0:HALO, cols]

        for lo in range(0, di, GROUP):
            cols = slice(lo, lo + GROUP)
            ee = ee_ref[:, cols]
            x = xc_ref[:, cols].astype(F32)
            dyb = dsc_ref[:, cols]
            dy = dyb.astype(F32)
            step_e = dot(step_2, ee)
            u = step_e * x
            ub = u.astype(BF)
            parts = []
            gap = dot(left, right[:, Q * (lo // width) : Q * ((lo + GROUP) // width)])
            for q in range(0, GROUP, 2 * width):
                pair = slice(q, q + 2 * width)
                dy_blocks = half_blocks(dyb[:, pair], width)
                d_m = dot_nt(ub[:, pair], dy_blocks)
                ms, ks = [], []
                first = (lo + q) // width
                for j in range(2):
                    h = first + j
                    at = Q * (h - lo // width)
                    fall = jnp.exp(jnp.minimum(gap[:, at : at + Q], 0.0))
                    m = mix_t * fall
                    d_one = d_m[:, Q * j : Q * (j + 1)]
                    d_mix = d_mix + d_one * fall
                    kb = (d_one * m).astype(BF)
                    kcol[h : h + 1, :] = jnp.sum(kb.astype(F32), axis=0, keepdims=True)
                    ms.append(m.astype(BF))
                    ks.append(kb)
                parts.append(dot(jnp.concatenate(ms, axis=1), dy_blocks))
                krow = krow + dot(jnp.concatenate(ks, axis=1), hot_ref[Q * first : Q * (first + 2), :])
            d_state = ds_state[:, cols]
            dsb = d_state.astype(BF)
            startb = start_ref[0, :, cols]
            tail_e = dot(tail_2, ee)
            from_state = tail_e * dot(bm, dsb)
            du = jnp.concatenate(parts, axis=1) + from_state
            edy = dot(ex_2, ee) * dy
            edyb = edy.astype(BF)
            d_b = d_b + dot_nt((tail_e * u).astype(BF), dsb)
            d_c = d_c + dot_nt(edyb, startb)
            three = jnp.concatenate([edy * dot(cm, startb), u * from_state, x * du], axis=0).astype(BF)
            sums = sums + dot(three, er_ref[cols, :])
            rows = jnp.concatenate(
                [
                    jnp.sum(startb.astype(F32) * d_state, axis=0, keepdims=True),
                    jnp.sum(dy * x, axis=0, keepdims=True),
                    jnp.zeros((6, GROUP), F32),
                ],
                axis=0,
            )
            rows_hi = rows.astype(BF)
            rows_lo = (rows - rows_hi.astype(F32)).astype(BF)
            row_sums = row_sums + dot(jnp.concatenate([rows_hi, rows_lo], axis=0), er_ref[cols, :])
            ds_state[:, cols] = dot(end_2, ee)[0:1] * d_state + dot_tn(cm, edyb)
            conv_back(cols, (step_e * du + skip_ref[:, cols] * dy) * slope_ref[:, cols].astype(F32))

        d_mixb = jnp.where(causal, d_mix, 0.0).astype(BF)
        d_bc = jnp.concatenate([d_b + dot(d_mixb, cm), d_c + dot_tn(d_mixb, bm)], axis=1)
        conv_back(slice(di, cd), d_bc * slope_ref[:, di:].astype(F32))
        upper = causal.astype(F32)
        strict = tri(Q, Q, lambda r, c: c < r).astype(F32)
        row_sums = row_sums[0:8] + row_sums[8:16]
        pairs = jnp.concatenate([kcol[...].T + sums[:Q] - krow, sums[Q : 2 * Q]], axis=0)
        d_decay = choose_sum(jnp.concatenate([upper, strict], axis=1), pairs) + at_end * row_sums[0:1]
        d_dt = (sums[2 * Q :] + nega * d_decay) * sigmoid(dtv)
        d_ref[:, cd:] = d_dt.astype(BF)
        ghead_ref[0:1, :] += jnp.sum(d_dt, axis=0, keepdims=True)
        ghead_ref[1:2, :] += jnp.sum(d_decay * nega * step, axis=0, keepdims=True)
        ghead_ref[2:3, :] += row_sums[1:2]

    @pl.when(i == n)
    def _():
        full_d[0:Q, :] = jnp.zeros((Q, cd), BF)
        cin = prev_ref[...].astype(F32)
        edge = jnp.zeros((HALO, cd), F32)
        for k in range(CONV - 1):
            later = dot(shift_ref[Q * (k + 1) - HALO : Q * (k + 1), :], full_d[...])
            edge = edge + tap(k) * later
            gconv_ref[k : k + 1, :] += jnp.sum(later * cin, axis=0, keepdims=True)
        d_ref[...] = jnp.zeros_like(d_ref)
        d_ref[Q - HALO :, :cd] = edge.astype(BF)


def stream_back_kernel(d_ref, dnz_ref, wa_ref, wb_ref, small_ref, s_ref, halo_ref, cot_ref, gs_ref, msg_ref):
    i = pl.program_id(0)
    d, ca = wa_ref.shape
    cdp = d_ref.shape[1]

    def through(dn, s):
        inv = root_of(s)
        weighted = small_ref[0:1, :d] * dn
        unit = s * inv
        return inv * (weighted - unit * jnp.mean(weighted * unit, axis=-1, keepdims=True))

    def back(rows):
        return dot_nt(rows[:, :ca], wa_ref[...]) + dot_nt(rows[:, ca:], wb_ref[:, : cdp - ca])

    @pl.when(i == 0)
    def _():
        msg_ref[...] = through(back(d_ref[Q - HALO :, :]), halo_ref[...])

    @pl.when(i > 0)
    def _():
        gs_ref[...] = cot_ref[...] + through(dnz_ref[...] + back(d_ref[...]), s_ref[...])


VMEM = pltpu.CompilerParams(vmem_limit_bytes=60 * 2**20)


def whole(a):
    return pl.BlockSpec(a.shape, lambda *_: (0,) * a.ndim)


def cost(flops, *arrays):
    return pl.CostEstimate(
        flops=int(flops), transcendentals=0, bytes_accessed=sum(a.size * a.dtype.itemsize for a in arrays)
    )


def shape(*dims, dtype=F32):
    return jax.ShapeDtypeStruct(dims, dtype)


def flip(v, axis, n, bit):
    return lax.ppermute(v, axis, [(s, s ^ bit) for s in range(n)])


def shift(v, axis, n, by):
    return lax.ppermute(v, axis, [(s, (s + by) % n) for s in range(n)])


def far_gather(v, n):
    far = n // 4
    z = lax.axis_index("seq") // 4
    got = [v] + [shift(v, "seq", n, 4 * k) for k in range(1, far)]
    buf = jnp.zeros((far,) + v.shape, v.dtype)
    for k in range(far):
        buf = lax.dynamic_update_slice_in_dim(buf, got[k][None], (z - k) % far, 0)
    return buf


def pair_gather(v, n, bit, axis):
    other = flip(v, "seq", n, bit)
    mine = (lax.axis_index("seq") // bit) % 2 == 0
    return jnp.where(mine, jnp.stack([v, other], axis), jnp.stack([other, v], axis))


def gather_rows(v, n, ca):
    a, b = v[:, :ca], v[:, ca:]
    b = pair_gather(b, n, 2, 0)
    a = far_gather(a, n)
    a = pair_gather(a, n, 2, 1)
    b = far_gather(b, n)
    a, b = pair_gather(a, n, 1, 2), pair_gather(b, n, 1, 2)
    return a.reshape(-1, a.shape[-1]), b.reshape(-1, b.shape[-1])


def pair_scatter(v, n, bit, axis):
    me = (lax.axis_index("seq") // bit) % 2
    mine = lax.dynamic_index_in_dim(v, me, axis, False)
    other = flip(lax.dynamic_index_in_dim(v, 1 - me, axis, False), "seq", n, bit)
    return (mine.astype(F32) + other.astype(F32)).astype(BF)


def far_scatter(v, n):
    far = n // 4
    z = lax.axis_index("seq") // 4
    total = lax.dynamic_index_in_dim(v, z, 0, False).astype(F32)
    for k in range(1, far):
        sent = lax.dynamic_index_in_dim(v, (z + k) % far, 0, False)
        total = total + shift(sent, "seq", n, 4 * k).astype(F32)
    return total.astype(BF)


def over_hx(v, hx):
    if hx == 2:
        b = v.astype(BF)
        return b.astype(F32) + flip(b, "hx", hx, 1).astype(F32)
    return lax.psum(v.astype(F32), "hx")


def sum_steps(n, hx):
    steps = []
    for axis, size in (("seq", n), ("hx", hx)):
        bit = 1
        while bit < size:
            steps.append(functools.partial(lambda axis, size, bit, v: v + flip(v, axis, size, bit), axis, size, bit))
            bit *= 2
    return steps


def together(*values):
    return lax.optimization_barrier(values)


def shards(
    stream,
    cotangent,
    norm_gain,
    in_main,
    in_dt,
    conv_weight,
    conv_bias,
    dt_bias,
    a_log,
    skip_gain,
    gated_gain,
    out_weight,
):
    n, hx = lax.axis_size("seq"), lax.axis_size("hx")
    s, cot = stream[0], cotangent[0]
    t, d = s.shape
    heads = in_dt.shape[1]
    di = out_weight.shape[0] * n
    cd = conv_weight.shape[1] * n
    width = di // heads
    nc = t // Q
    cdp = cd + LANES
    rows = in_main.shape[0]
    per = di // d

    def lanes(v):
        return jnp.pad(v, ((0, 0), (0, LANES - v.shape[1])))

    small = jnp.concatenate(
        [lanes(norm_gain[None]), lanes(conv_weight), lanes(conv_bias[None]), lanes(gated_gain[None])], axis=0
    )
    small = jnp.pad(small, ((0, rows - small.shape[0]), (0, 0)))
    wx = jnp.concatenate([in_main[:, di:], lanes(in_dt), small], axis=1)
    ca = wx.shape[1] * 2 // 3 // GROUP * GROUP
    wa, wb = gather_rows(wx, n, ca)
    wzo = jnp.concatenate([in_main[:, :di], out_weight.reshape(per, rows, d).transpose(1, 0, 2).reshape(rows, di)], axis=1)
    wzo = lax.all_gather(wzo, "seq", axis=0, tiled=True)
    halo = lax.ppermute(s[t - HALO :], "hx", [(r, r + 1) for r in range(hx - 1)])

    head_rows = jnp.pad(jnp.stack([dt_bias, -jnp.exp(a_log)]), ((0, 6), (0, LANES - heads)))
    owner = jnp.arange(di, dtype=jnp.int32) // width
    er = (owner[:, None] == jnp.arange(LANES, dtype=jnp.int32)[None, :]).astype(BF)
    one = (jnp.arange(LANES, dtype=jnp.int32)[:, None] == owner[None, :]).astype(BF)
    ee = jnp.concatenate([one, one], axis=0)
    skip = jnp.repeat(skip_gain, width)[None, :]
    hot = (
        (jnp.arange(heads * Q, dtype=jnp.int32) // Q)[:, None] == jnp.arange(LANES, dtype=jnp.int32)[None, :]
    ).astype(BF)

    block = jnp.arange(heads * Q, dtype=jnp.int32) // Q
    which = jnp.arange(LANES, dtype=jnp.int32)
    pick = ((which[:, None] % 32 == block[None, :]) & (which[:, None] < 96)).astype(BF)
    row = jnp.arange((CONV - 1) * Q, dtype=jnp.int32)[:, None]
    col = jnp.arange(Q + HALO, dtype=jnp.int32)[None, :]
    ahead = (col == HALO + row % Q - (CONV - 1) + row // Q).astype(BF)
    behind = (col == row % Q + (CONV - 1) - row // Q).astype(BF)
    nw = t // WIDE
    two = WIDE // Q

    def at(i):
        return jnp.maximum(i - 1, 0)

    wa, er, ee, skip, hot, pick, ahead, behind = together(wa, er, ee, skip, hot, pick, ahead, behind)
    args = (halo, s, wa, wb, head_rows, ee, ahead)
    nrm, cin, xc, slope, dtv, cum, base, sloc, fin, tot, small = pl.pallas_call(
        functools.partial(project_kernel, n),
        grid=(nw + 1,),
        in_specs=[whole(halo), pl.BlockSpec((WIDE, d), lambda i: (at(i), 0))] + [whole(a) for a in args[2:]],
        out_specs=[
            pl.BlockSpec((WIDE, d), lambda i: (i, 0)),
            pl.BlockSpec((WIDE, cd), lambda i: (i, 0)),
            pl.BlockSpec((WIDE, cd), lambda i: (at(i), 0)),
            pl.BlockSpec((WIDE, cd), lambda i: (at(i), 0)),
            pl.BlockSpec((WIDE, LANES), lambda i: (at(i), 0)),
            pl.BlockSpec((WIDE, LANES), lambda i: (at(i), 0)),
            pl.BlockSpec((8 * two, LANES), lambda i: (at(i), 0)),
            pl.BlockSpec((two, STATE, di), lambda i: (at(i), 0, 0)),
            pl.BlockSpec((STATE, di), lambda i: (0, 0)),
            pl.BlockSpec((8, LANES), lambda i: (0, 0)),
            pl.BlockSpec((8, cd), lambda i: (0, 0)),
        ],
        out_shape=[
            shape(t + WIDE, d, dtype=BF),
            shape(t + WIDE, cd, dtype=BF),
            shape(t, cd, dtype=BF),
            shape(t, cd, dtype=BF),
            shape(t, LANES),
            shape(t, LANES),
            shape(8 * nc, LANES),
            shape(nc, STATE, di, dtype=BF),
            shape(STATE, di, dtype=BF),
            shape(8, LANES),
            shape(8, cd),
        ],
        scratch_shapes=[pltpu.VMEM((WIDE + HALO, cd), BF), pltpu.VMEM((STATE, di), F32), pltpu.VMEM((8, LANES), F32)],
        compiler_params=VMEM,
        cost_estimate=cost(3 * t * d * cdp, s, wa, wb, s, s),
        name="project",
    )(*args)

    def carry(v, step_by):
        links = [(r, r + step_by) for r in range(hx) if 0 <= r + step_by < hx]
        got = lax.ppermute(v, "hx", links)
        total = got
        if hx > 2:
            fade = jnp.repeat(jnp.exp(tot[0, :heads]), width)[None, :]
            total = got.astype(F32)
            for _ in range(hx - 2):
                got = lax.ppermute((fade * got.astype(F32)).astype(BF), "hx", links)
                total = total + got.astype(F32)
            total = total.astype(BF)
        return total

    hin = carry(fin, 1)

    args = (xc, dtv, cum, skip, ee, pick)
    yi = pl.pallas_call(
        functools.partial(intra_kernel, width),
        grid=(nc,),
        in_specs=[
            pl.BlockSpec((Q, cd), lambda i: (i, 0)),
            pl.BlockSpec((Q, LANES), lambda i: (i, 0)),
            pl.BlockSpec((Q, LANES), lambda i: (i, 0)),
            whole(skip),
            whole(ee),
            whole(pick),
        ],
        out_specs=pl.BlockSpec((Q, di), lambda i: (i, 0)),
        out_shape=shape(t, di, dtype=BF),
        scratch_shapes=[pltpu.VMEM(pick.shape, BF)],
        compiler_params=VMEM,
        cost_estimate=cost(2 * t * d * di, xc, xc),
        name="intra",
    )(*args)

    args = (yi, nrm, xc, cum, base, sloc, hin, s, cot, wzo, small, ee)
    out, mixed, dsc, dz, start, gst = pl.pallas_call(
        functools.partial(gate_kernel, n),
        grid=(nw,),
        in_specs=[
            pl.BlockSpec((WIDE, di), lambda i: (i, 0)),
            pl.BlockSpec((WIDE, d), lambda i: (i + 1, 0)),
            pl.BlockSpec((WIDE, STATE), lambda i: (i, cd // STATE - 1)),
            pl.BlockSpec((WIDE, LANES), lambda i: (i, 0)),
            pl.BlockSpec((8 * two, LANES), lambda i: (i, 0)),
            pl.BlockSpec((two, STATE, di), lambda i: (i, 0, 0)),
            whole(hin),
            pl.BlockSpec((WIDE, d), lambda i: (i, 0)),
            pl.BlockSpec((WIDE, d), lambda i: (i, 0)),
            whole(wzo),
            whole(small),
            whole(ee),
        ],
        out_specs=[
            pl.BlockSpec((WIDE, d), lambda i: (i, 0)),
            pl.BlockSpec((WIDE, di), lambda i: (i, 0)),
            pl.BlockSpec((WIDE, di), lambda i: (i, 0)),
            pl.BlockSpec((WIDE, di), lambda i: (i, 0)),
            pl.BlockSpec((two, STATE, di), lambda i: (i, 0, 0)),
            pl.BlockSpec((STATE, di), lambda i: (0, 0)),
        ],
        out_shape=[
            shape(t, d),
            shape(t, di, dtype=BF),
            shape(t, di, dtype=BF),
            shape(t, di, dtype=BF),
            shape(nc, STATE, di, dtype=BF),
            shape(STATE, di, dtype=BF),
        ],
        scratch_shapes=[
            pltpu.VMEM((STATE, di), F32),
            pltpu.VMEM((di, d), BF),
            pltpu.VMEM((WIDE, di), BF),
            pltpu.VMEM((WIDE, di), F32),
            pltpu.VMEM((WIDE, di), F32),
        ],
        compiler_params=VMEM,
        cost_estimate=cost(6 * t * d * di, yi, yi, yi, xc, s, s, s),
        name="gate",
    )(*args)

    gin = carry(gst, -1)
    g_z = dot_tn(nrm[WIDE:], dz).astype(BF)
    g_out = dot_tn(mixed, cot.astype(BF)).astype(BF)
    g_zo = [g_z[:, d * k : d * (k + 1)].reshape(n, rows, d) for k in range(per)] + [g_out.reshape(n, rows * per, d)]
    g_zo = jnp.concatenate(g_zo, axis=1).reshape(2 * di, d)
    g_zo = lax.psum_scatter(g_zo, "seq", scatter_dimension=0, tiled=True)
    args = (xc, slope, dtv, cum, start, gin, dsc, cin, cin, small, head_rows, skip, ee, er, hot, pick, behind)

    def back(i):
        return jnp.maximum(nc - 1 - i, 0)

    dx, gconv, ghead = pl.pallas_call(
        functools.partial(scan_back_kernel, width),
        grid=(nc + 1,),
        in_specs=[
            pl.BlockSpec((Q, cd), lambda i: (back(i), 0)),
            pl.BlockSpec((Q, cd), lambda i: (back(i), 0)),
            pl.BlockSpec((Q, LANES), lambda i: (back(i), 0)),
            pl.BlockSpec((Q, LANES), lambda i: (back(i), 0)),
            pl.BlockSpec((1, STATE, di), lambda i: (back(i), 0, 0)),
            whole(gin),
            pl.BlockSpec((Q, di), lambda i: (back(i), 0)),
            pl.BlockSpec((Q, cd), lambda i: (back(i) + two, 0)),
            pl.BlockSpec((HALO, cd), lambda i: (WIDE // HALO - 1, 0)),
        ]
        + [whole(a) for a in args[9:]],
        out_specs=[
            pl.BlockSpec((Q, cdp), lambda i: (nc - i, 0)),
            pl.BlockSpec((8, cd), lambda i: (0, 0)),
            pl.BlockSpec((8, LANES), lambda i: (0, 0)),
        ],
        out_shape=[shape(t + Q, cdp, dtype=BF), shape(8, cd), shape(8, LANES)],
        scratch_shapes=[
            pltpu.VMEM((Q + HALO, cd), BF),
            pltpu.VMEM((STATE, di), F32),
            pltpu.VMEM((LANES, Q), F32),
            pltpu.VMEM(pick.shape, BF),
        ],
        compiler_params=VMEM,
        cost_estimate=cost(8 * t * d * di, xc, xc, xc, xc),
        name="scan_back",
    )(*args)

    packed = jnp.concatenate([gconv, jnp.pad(ghead, ((0, 0), (0, LANES)))], axis=1)
    steps = sum_steps(n, hx)
    packed = steps[0](packed)
    g_x = dot_tn(nrm[WIDE - Q :], dx).astype(BF)
    g_x, dz, packed = together(g_x, dz, packed)
    g_x = pair_scatter(g_x.reshape(n // 4, 2, 2, rows, cdp), n, 1, 2)
    packed = steps[1](packed)
    dnz = dot_nt(dz, wzo[:, :di])
    g_x, packed, dnz, dx = together(g_x, packed, dnz, dx)
    g_x = pair_scatter(g_x, n, 2, 1)
    packed = steps[2](packed)

    args = (dx, dnz, wa, wb, small, s, halo, cot)
    g_stream, msg = pl.pallas_call(
        stream_back_kernel,
        grid=(nc + 1,),
        in_specs=[
            pl.BlockSpec((Q, cdp), lambda i: (i, 0)),
            pl.BlockSpec((Q, d), lambda i: (at(i), 0)),
            whole(wa),
            whole(wb),
            whole(small),
            pl.BlockSpec((Q, d), lambda i: (at(i), 0)),
            whole(halo),
            pl.BlockSpec((Q, d), lambda i: (at(i), 0)),
        ],
        out_specs=[pl.BlockSpec((Q, d), lambda i: (at(i), 0)), pl.BlockSpec((HALO, d), lambda i: (0, 0))],
        out_shape=[shape(t, d), shape(HALO, d)],
        compiler_params=VMEM,
        cost_estimate=cost(2 * t * d * cdp, s, s, s, s, wa, wb),
        name="stream_back",
    )(*args)
    g_x, packed, msg, g_zo = together(g_x, packed, msg, g_zo)
    g_zo = over_hx(g_zo, hx)
    msg = lax.ppermute(msg, "hx", [(r + 1, r) for r in range(hx - 1)])
    g_x = far_scatter(g_x, n)
    for step in steps[3:-1]:
        packed = step(packed)
    g_x = over_hx(g_x, hx)
    packed = steps[-1](packed)
    g_stream = lax.dynamic_update_slice(g_stream, g_stream[t - HALO :] + msg, (t - HALO, 0))
    mine = lax.dynamic_slice_in_dim(packed[:, :cd], lax.axis_index("seq") * (cd // n), cd // n, 1)
    g_z = jnp.concatenate([g_zo[rows * k : rows * (k + 1)] for k in range(per)], axis=1)
    g_out = g_zo[rows * per :]
    g_main = jnp.concatenate([g_z, g_x[:, :cd]], axis=1)
    g_dt = g_x[:, cd : cd + heads]
    g_norm = (
        jnp.sum(in_main.astype(F32) * g_main, axis=1) + jnp.sum(in_dt.astype(F32) * g_dt, axis=1)
    ) / norm_gain.astype(F32)
    g_gate = jnp.sum(out_weight.astype(F32) * g_out, axis=1) / gated_gain.astype(F32)
    return (
        out[None],
        g_stream[None],
        g_norm,
        g_main,
        g_dt,
        mine[:CONV],
        mine[CONV],
        packed[0, cd : cd + heads],
        packed[1, cd : cd + heads],
        packed[2, cd : cd + heads],
        g_gate,
        g_out,
    )


def solution(mesh):
    placed = (
        P("seq", "hx", None),
        P("seq", "hx", None),
        P("seq"),
        P("seq", None),
        P("seq", None),
        P(None, "seq"),
        P("seq"),
        P(),
        P(),
        P(),
        P("seq"),
        P("seq", None),
    )
    return jax.shard_map(
        shards,
        mesh=mesh,
        in_specs=placed,
        out_specs=(
            P("seq", "hx", None),
            P("seq", "hx", None),
            P("seq"),
            P("seq", None),
            P("seq", None),
            P(None, "seq"),
            P("seq"),
            P(),
            P(),
            P(),
            P("seq"),
            P("seq", None),
        ),
        check_vma=False,
    )
```
